128 devices in a mesh: pairs: 32 (over y, z, core), items: 4 (over x).
Axes of the slice: x: 4, y: 4, z: 4, core: 2. Of those that a mesh axis runs over, the one named last changes fastest.
Arguments:
- user_table: bfloat16 [131072, 1024], P(('pairs', 'items'))
- item_table: bfloat16 [8192, 1024], P('items')
- pair_user: int32 [262144], P(('pairs', 'items')), may hold values from 0 to 1023
- pair_item: int32 [262144], P(('pairs', 'items')), may hold values from 0 to 2047
- pair_owner: int32 [262144], P(('pairs', 'items')), may hold values from 0 to 3, as said below
- pair_count: int32 [128], P(('pairs', 'items')), may hold values from 1024 to 2048, as said below
Outputs:
- r_user: float32 [1024, 1024], replicated
- r_item: float32 [1024, 1024], replicated
- whitened: float32 [1024, 1024], P(('pairs', 'items'))
The draws below stay inside these ranges and needn't reach their ends.
Inputs may be any that keep to these rules, and one draw needn't show every extreme that they name: `pair_owner`: among the 2048 pair slots of one device at most 1024 name one owner; in every group of devices along items one owner is named by exactly 1024 slots of every device of the group. `pair_count`: some device has all 2048 slots valid.
All inputs are finite; a program needn't handle non-finite values.
Results may differ from the reference program's by a relative error of at most 0.0003.
Values may be sent and summed in bfloat16 or wider, within the bound.
No kernel may reach another device: no remote copies, remote signals or barrier semaphores. Data moves between devices by JAX's collectives and lax.ppermute only.
A program may use at most 128 MiB of HBM per device.

```python
import jax
import jax.numpy as jnp
from jax import lax

D = 1024
PAIR_DEV = 2048
ITEM_DEV = 2048
USER_DEV = 1024
CAP = 1024
PAIRS = 262144
USERS = 131072
ITEMS = 8192
N_ITEMS = 4
DEVICES = 128


def scaled_table(key, rows):
    kbase, krow, kcol = jax.random.split(key, 3)
    base = jax.random.normal(kbase, (rows, D), jnp.float32)
    row_scale = jnp.exp(jax.random.uniform(krow, (rows, 1), jnp.float32, -1.15, 1.15))
    col_scale = jnp.exp(jax.random.uniform(kcol, (1, D), jnp.float32, -1.15, 1.15))
    return (base * row_scale * col_scale * 0.5).astype(jnp.bfloat16)


def draw_user_table(key, part):
    return scaled_table(jax.random.fold_in(key, 11), USERS)


def draw_item_table(key, part):
    return scaled_table(jax.random.fold_in(key, 23), ITEMS)


def draw_pair_owner(key, part):
    kheavy, krest, kperm = jax.random.split(jax.random.fold_in(key, 37), 3)
    groups = DEVICES // N_ITEMS
    heavy = jax.random.randint(kheavy, (groups,), 0, N_ITEMS, dtype=jnp.int32)
    heavy_dev = jnp.repeat(heavy, N_ITEMS)
    rest = jax.random.randint(krest, (DEVICES, PAIR_DEV - CAP), 0, N_ITEMS - 1, dtype=jnp.int32)
    rest = rest + (rest >= heavy_dev[:, None]).astype(jnp.int32)
    first = jnp.broadcast_to(heavy_dev[:, None], (DEVICES, CAP))
    owners = jnp.concatenate([first, rest], axis=1)
    keys = jax.random.split(kperm, DEVICES)
    orders = jax.vmap(lambda k: jax.random.permutation(k, PAIR_DEV))(keys)
    owners = jnp.take_along_axis(owners, orders.astype(jnp.int32), axis=1)
    return owners.reshape(-1).astype(jnp.int32)


def draw_pair_count(key, part):
    kcount, kpick = jax.random.split(jax.random.fold_in(key, 53))
    counts = jax.random.randint(kcount, (DEVICES,), PAIR_DEV // 2, PAIR_DEV + 1, dtype=jnp.int32)
    chosen = jax.random.randint(kpick, (), 0, DEVICES, dtype=jnp.int32)
    return jnp.where(jnp.arange(DEVICES, dtype=jnp.int32) == chosen, PAIR_DEV, counts).astype(jnp.int32)


def touch_ends(drawn, stream_key, least, largest):
    longest = drawn.shape.index(max(drawn.shape))
    spots = []
    for shift in (0, 1):
        where = [jax.random.randint(jax.random.fold_in(stream_key, axis), (), 0, length) for axis, length in enumerate(drawn.shape)]
        where[longest] = (where[longest] + shift) % drawn.shape[longest]
        spots.append(tuple(where))
    return drawn.at[spots[0]].set(least).at[spots[1]].set(largest)


def setup_inputs(seed: int = 0) -> dict:
    splits = jax.random.split(jax.random.key(seed), 7)
    return {
        "user_table": draw_user_table(jax.random.fold_in(splits[6], 71), 0),
        "item_table": draw_item_table(jax.random.fold_in(splits[6], 71), 0),
        "pair_user": touch_ends(jax.random.randint(splits[2], (PAIRS,), 0, USER_DEV), jax.random.fold_in(splits[2], 1), 0, USER_DEV - 1).astype(jnp.int32),
        "pair_item": touch_ends(jax.random.randint(splits[3], (PAIRS,), 0, ITEM_DEV), jax.random.fold_in(splits[3], 1), 0, ITEM_DEV - 1).astype(jnp.int32),
        "pair_owner": draw_pair_owner(jax.random.fold_in(splits[6], 71), 0),
        "pair_count": draw_pair_count(jax.random.fold_in(splits[6], 71), 0),
    }


def reference(user_table, item_table, pair_user, pair_item, pair_owner, pair_count):
    users = user_table.reshape(DEVICES, USER_DEV, D)
    user_ids = pair_user.reshape(DEVICES, PAIR_DEV)
    item_ids = (pair_owner * ITEM_DEV + pair_item).reshape(DEVICES, PAIR_DEV)
    slots = jnp.arange(PAIR_DEV, dtype=jnp.int32)
    zero_sq = jnp.zeros((D, D), jnp.float32)

    def accumulate(carry, device):
        gram_user, gram_item, cross = carry
        keep = (slots < pair_count[device])[:, None]
        upanel = jnp.where(keep, jnp.take(users[device], user_ids[device], axis=0), jnp.zeros((), jnp.bfloat16))
        ipanel = jnp.where(keep, jnp.take(item_table, item_ids[device], axis=0), jnp.zeros((), jnp.bfloat16))
        dims = (((0,), (0,)), ((), ()))
        gram_user = gram_user + lax.dot_general(upanel.astype(jnp.float32), upanel.astype(jnp.float32), dims, preferred_element_type=jnp.float32)
        gram_item = gram_item + lax.dot_general(ipanel.astype(jnp.float32), ipanel.astype(jnp.float32), dims, preferred_element_type=jnp.float32)
        cross = cross + lax.dot_general(upanel.astype(jnp.float32), ipanel.astype(jnp.float32), dims, preferred_element_type=jnp.float32)
        return ((gram_user, gram_item, cross), None)
    devices = jnp.arange(DEVICES, dtype=jnp.int32)
    (gram_user, gram_item, cross), unused = lax.scan(accumulate, (zero_sq, zero_sq, zero_sq), devices)
    total = float(PAIRS)
    lower_user = jnp.linalg.cholesky(gram_user / total)
    lower_item = jnp.linalg.cholesky(gram_item / total)
    left = jax.scipy.linalg.solve_triangular(lower_user, cross / total, lower=True)
    whitened = jax.scipy.linalg.solve_triangular(lower_item, left.T, lower=True).T * jnp.sqrt(jnp.float32(total))
    return (lower_user.T, lower_item.T, whitened)
```

```python
import jax
import jax.numpy as jnp
from jax import lax
from jax.experimental import pallas as pl
from jax.experimental.pallas import tpu as pltpu
from jax.sharding import PartitionSpec as P

N = 1024
NB = 128
KB = N // NB
SUB = 32
HI = lax.Precision.HIGHEST
F32 = jnp.float32


def row_of(v, t):
    return jnp.broadcast_to(v[t:t + 1, :], v.shape)


def lane_of(v, c):
    return jnp.broadcast_to(v[:, c:c + 1], (8, NB))


def dot(a, b, ca, cb):
    return lax.dot_general(a, b, (((ca,), (cb,)), ((), ())), precision=HI, preferred_element_type=F32)


def factor(refs):
    sub = lax.broadcasted_iota(jnp.int32, (8, NB), 0)
    groups = SUB // 8
    for s in range(NB // SUB):
        panels = [[(r[SUB * s + 8 * g:SUB * s + 8 * g + 8, :NB], r[SUB * s + 8 * g:SUB * s + 8 * g + 8, NB:]) for g in range(groups)] for r in refs]
        for g in range(groups):
            for m, r in enumerate(refs):
                base = SUB * s + 8 * g
                left, right = panels[m][g]
                cols = [lane_of(left, base + t) for t in range(8)]
                fac = [[None] * 8 for _ in range(8)]
                inv = []
                rows_l, rows_r = [], []
                for t in range(8):
                    d = row_of(cols[t], t)
                    ri = lax.rsqrt(d)
                    inv.append(ri)
                    lt = cols[t] * ri
                    for u in range(t + 1, 8):
                        fac[t][u] = row_of(lt, u)
                        cols[u] = cols[u] - lt * fac[t][u]
                    pl_, pr_ = row_of(left, t), row_of(right, t)
                    for k in range(t):
                        pl_ = pl_ - fac[k][t] * rows_l[k]
                        pr_ = pr_ - fac[k][t] * rows_r[k]
                    rows_l.append(pl_ * ri)
                    rows_r.append(pr_ * ri)
                for h in range(g + 1, groups):
                    hl, hr = panels[m][h]
                    hc = [lane_of(hl, base + t) for t in range(8)]
                    for t in range(8):
                        ht = hc[t] * inv[t]
                        for u in range(t + 1, 8):
                            hc[u] = hc[u] - ht * fac[t][u]
                        hl = hl - ht * rows_l[t]
                        hr = hr - ht * rows_r[t]
                    panels[m][h] = (hl, hr)
                out_l, out_r = rows_l[0], rows_r[0]
                for t in range(1, 8):
                    out_l = jnp.where(sub == t, rows_l[t], out_l)
                    out_r = jnp.where(sub == t, rows_r[t], out_r)
                r[base:base + 8, :NB] = out_l
                r[base:base + 8, NB:] = out_r
        lo = SUB * (s + 1)
        if lo < NB:
            for r in refs:
                got = r[SUB * s:lo, :]
                r[lo:, :] = r[lo:, :] - dot(got[:, lo:NB], got, 0, 0)


def chol_kernel(gu_ref, gi_ref, ru_ref, ri_ref, wu_ref, wi_ref, au, ai):
    scale = F32(1.0)
    row = lax.broadcasted_iota(jnp.int32, (NB, NB), 0)
    col = lax.broadcasted_iota(jnp.int32, (NB, NB), 1)
    eye = (row == col).astype(F32)
    pairs = ((gu_ref, ru_ref, wu_ref, au), (gi_ref, ri_ref, wi_ref, ai))
    for g, r, w, a in pairs:
        r[...] = g[...]

    def step(k, _):
        at = pl.multiple_of(k * NB, NB)
        for g, r, w, a in pairs:
            a[:, :NB] = r[pl.ds(at, NB), pl.ds(at, NB)]
            a[:, NB:] = eye
        factor([p[3] for p in pairs])
        for g, r, w, a in pairs:
            w[pl.ds(at, NB), :] = a[:, NB:]
            r[pl.ds(at, NB), pl.ds(at, NB)] = jnp.where(col >= row, a[:, :NB], 0.0)

        def panel(j, _):
            to = pl.multiple_of(j * NB, NB)
            for g, r, w, a in pairs:
                r[pl.ds(at, NB), pl.ds(to, NB)] = dot(a[:, NB:], r[pl.ds(at, NB), pl.ds(to, NB)], 1, 0)
            return 0
        lax.fori_loop(k + 1, KB, panel, 0)

        def zero(j, _):
            to = pl.multiple_of(j * NB, NB)
            for g, r, w, a in pairs:
                r[pl.ds(at, NB), pl.ds(to, NB)] = jnp.zeros((NB, NB), F32)
            return 0
        lax.fori_loop(0, k, zero, 0)

        def outer(i, _):
            ri = pl.multiple_of(i * NB, NB)

            def inner(j, _):
                to = pl.multiple_of(j * NB, NB)
                for g, r, w, a in pairs:
                    r[pl.ds(ri, NB), pl.ds(to, NB)] = r[pl.ds(ri, NB), pl.ds(to, NB)] - dot(r[pl.ds(at, NB), pl.ds(ri, NB)], r[pl.ds(at, NB), pl.ds(to, NB)], 0, 0)
                return 0
            lax.fori_loop(i, KB, inner, 0)
            return 0
        lax.fori_loop(k + 1, KB, outer, 0)
        return 0

    lax.fori_loop(0, KB, step, 0)


def chol2(gu, gi):
    full = jax.ShapeDtypeStruct((N, N), F32)
    inv = jax.ShapeDtypeStruct((N, NB), F32)
    vm = pl.BlockSpec(memory_space=pltpu.VMEM)
    return pl.pallas_call(
        chol_kernel,
        out_shape=(full, full, inv, inv),
        in_specs=[vm, vm],
        out_specs=(vm, vm, vm, vm),
        scratch_shapes=[pltpu.VMEM((NB, 2 * NB), F32)] * 2,
        compiler_params=pltpu.CompilerParams(vmem_limit_bytes=48 << 20),
        name="chol_pair",
    )(gu, gi)


def thin_kernel(e_ref, c_ref, ru_ref, ri_ref, wu_ref, wi_ref, out_ref, x, y):
    x[...] = e_ref[...]
    for k in range(KB - 1, -1, -1):
        lo, hi = k * NB, (k + 1) * NB
        xk = dot(x[:, lo:hi], wu_ref[lo:hi, :], 1, 0)
        x[:, lo:hi] = xk
        if k:
            x[:, :lo] = x[:, :lo] - dot(xk, ru_ref[:lo, lo:hi], 1, 1)
    y[...] = dot(x[...], c_ref[...], 1, 0)
    for k in range(KB):
        lo, hi = k * NB, (k + 1) * NB
        yk = dot(y[:, lo:hi], wi_ref[lo:hi, :], 1, 1)
        out_ref[:, lo:hi] = yk
        if hi < N:
            y[:, hi:] = y[:, hi:] - dot(yk, ri_ref[lo:hi, hi:], 1, 0)


def thin(e, c, ru, ri, wu, wi):
    vm = pl.BlockSpec(memory_space=pltpu.VMEM)
    return pl.pallas_call(
        thin_kernel,
        out_shape=jax.ShapeDtypeStruct(e.shape, F32),
        in_specs=[vm] * 6,
        out_specs=vm,
        scratch_shapes=[pltpu.VMEM(e.shape, F32)] * 2,
        compiler_params=pltpu.CompilerParams(vmem_limit_bytes=48 << 20),
        name="thin",
    )(e, c, ru, ri, wu, wi)


def body(user_table, item_table, pair_user, pair_item, pair_owner, pair_count):
    owners = lax.axis_size("items")
    devices = lax.axis_size("pairs") * owners
    slots_dev = pair_owner.shape[0]
    width = user_table.shape[1]
    total = float(slots_dev * devices)
    capacity = slots_dev // 2
    onehot = (pair_owner[:, None] == jnp.arange(owners, dtype=jnp.int32)[None, :]).astype(jnp.int32)
    ranks = jnp.sum(onehot * (jnp.cumsum(onehot, axis=0) - 1), axis=1)
    flat_slot = pair_owner * capacity + ranks
    request = jnp.zeros((owners * capacity,), jnp.int32).at[flat_slot].set(pair_item)
    request = request.reshape(owners, capacity)
    wanted = lax.all_to_all(request, "items", split_axis=0, concat_axis=0, tiled=True)
    rows = jnp.take(item_table, wanted.reshape(-1), axis=0)
    rows = rows.reshape(wanted.shape[0], wanted.shape[1], width)
    fetched = lax.all_to_all(rows, "items", split_axis=0, concat_axis=0, tiled=True)
    item_raw = jnp.take(fetched.reshape(owners * capacity, width), flat_slot, axis=0)
    keep = (jnp.arange(slots_dev, dtype=jnp.int32) < pair_count[0])[:, None]
    user_raw = jnp.take(user_table, pair_user, axis=0)
    user_panel = jnp.where(keep, user_raw, jnp.zeros((), jnp.bfloat16))
    item_panel = jnp.where(keep, item_raw, jnp.zeros((), jnp.bfloat16))
    dims = (((0,), (0,)), ((), ()))
    gram_user = lax.dot_general(user_panel, user_panel, dims, preferred_element_type=jnp.float32)
    gram_item = lax.dot_general(item_panel, item_panel, dims, preferred_element_type=jnp.float32)
    cross = lax.dot_general(user_panel, item_panel, dims, preferred_element_type=jnp.float32)
    rows_out = width // devices
    root_total = jnp.sqrt(jnp.float32(total))
    gram_user, gram_item, cross = lax.psum((gram_user, gram_item, cross), ("pairs", "items"))
    r_user, r_item, inv_user, inv_item = chol2(gram_user / total, gram_item / total)
    position = lax.axis_index(("pairs", "items"))
    rows = lax.broadcasted_iota(jnp.int32, (rows_out, width), 0) + position * rows_out
    pick = (rows == lax.broadcasted_iota(jnp.int32, (rows_out, width), 1)).astype(F32)
    whitened = thin(pick, cross / total, r_user, r_item, inv_user, inv_item) * root_total
    return (r_user, r_item, whitened)


def solution(mesh):
    placed = (
        P(("pairs", "items"), None),
        P("items", None),
        P(("pairs", "items")),
        P(("pairs", "items")),
        P(("pairs", "items")),
        P(("pairs", "items")),
    )
    return jax.shard_map(
        body,
        mesh=mesh,
        in_specs=placed,
        out_specs=(P(), P(), P(("pairs", "items"), None)),
        check_vma=False,
    )
```

```python
import jax
import jax.numpy as jnp
from jax import lax
from jax.experimental import pallas as pl
from jax.experimental.pallas import tpu as pltpu
from jax.sharding import Mesh, PartitionSpec as P

N = 1024
NB = 128
KB = N // NB
SUB = 32
HI = lax.Precision.HIGHEST
F32 = jnp.float32
BF16 = jnp.bfloat16
ALL = ("y", "z", "core", "x")
PAIRS_OF = [(i, j) for i in range(KB) for j in range(i, KB)]
START = {ij: NB * n for n, ij in enumerate(PAIRS_OF)}


def row_of(v, t):
    return jnp.broadcast_to(v[t:t + 1, :], v.shape)


def lane_of(v, c):
    return jnp.broadcast_to(v[:, c:c + 1], (8, NB))


def dot(a, b, ca, cb):
    return lax.dot_general(a, b, (((ca,), (cb,)), ((), ())), precision=HI, preferred_element_type=F32)


def factor(refs):
    sub = lax.broadcasted_iota(jnp.int32, (8, NB), 0)
    groups = SUB // 8
    for s in range(NB // SUB):
        panels = [[(r[SUB * s + 8 * g:SUB * s + 8 * g + 8, :NB], r[SUB * s + 8 * g:SUB * s + 8 * g + 8, NB:]) for g in range(groups)] for r in refs]
        for g in range(groups):
            for m, r in enumerate(refs):
                base = SUB * s + 8 * g
                left, right = panels[m][g]
                cols = [lane_of(left, base + t) for t in range(8)]
                fac = [[None] * 8 for _ in range(8)]
                inv = []
                rows_l, rows_r = [], []
                for t in range(8):
                    d = row_of(cols[t], t)
                    ri = lax.rsqrt(d)
                    inv.append(ri)
                    lt = cols[t] * ri
                    for u in range(t + 1, 8):
                        fac[t][u] = row_of(lt, u)
                        cols[u] = cols[u] - lt * fac[t][u]
                    pl_, pr_ = row_of(left, t), row_of(right, t)
                    for k in range(t):
                        pl_ = pl_ - fac[k][t] * rows_l[k]
                        pr_ = pr_ - fac[k][t] * rows_r[k]
                    rows_l.append(pl_ * ri)
                    rows_r.append(pr_ * ri)
                for h in range(g + 1, groups):
                    hl, hr = panels[m][h]
                    hc = [lane_of(hl, base + t) for t in range(8)]
                    for t in range(8):
                        ht = hc[t] * inv[t]
                        for u in range(t + 1, 8):
                            hc[u] = hc[u] - ht * fac[t][u]
                        hl = hl - ht * rows_l[t]
                        hr = hr - ht * rows_r[t]
                    panels[m][h] = (hl, hr)
                out_l, out_r = rows_l[0], rows_r[0]
                for t in range(1, 8):
                    out_l = jnp.where(sub == t, rows_l[t], out_l)
                    out_r = jnp.where(sub == t, rows_r[t], out_r)
                r[base:base + 8, :NB] = out_l
                r[base:base + 8, NB:] = out_r
        lo = SUB * (s + 1)
        if lo < NB:
            for r in refs:
                got = r[SUB * s:lo, :]
                r[lo:, :] = r[lo:, :] - dot(got[:, lo:NB], got, 0, 0)


def chol_kernel(scale, g_ref, r_ref, w_ref, a):
    row = lax.broadcasted_iota(jnp.int32, (NB, NB), 0)
    col = lax.broadcasted_iota(jnp.int32, (NB, NB), 1)
    eye = (row == col).astype(F32)
    for i in range(KB):
        if i:
            r_ref[NB * i:NB * (i + 1), :NB * i] = jnp.zeros((NB, NB * i), F32)
        for j in range(i, KB):
            at = START[i, j]
            r_ref[NB * i:NB * (i + 1), NB * j:NB * (j + 1)] = g_ref[at:at + NB, :] * scale

    def step(k, _):
        at = pl.multiple_of(k * NB, NB)
        here = pl.ds(at, NB)
        a[:, :NB] = r_ref[here, here]
        a[:, NB:] = eye
        factor([a])
        w_ref[here, :] = a[:, NB:]
        r_ref[here, here] = jnp.where(col >= row, a[:, :NB], 0.0)

        def panel(j, _):
            there = pl.ds(pl.multiple_of(j * NB, NB), NB)
            r_ref[here, there] = dot(a[:, NB:], r_ref[here, there], 1, 0)
            return 0
        lax.fori_loop(k + 1, KB, panel, 0)

        def outer(i, _):
            mine = pl.ds(pl.multiple_of(i * NB, NB), NB)

            def inner(j, _):
                there = pl.ds(pl.multiple_of(j * NB, NB), NB)
                r_ref[mine, there] = r_ref[mine, there] - dot(r_ref[here, mine], r_ref[here, there], 0, 0)
                return 0
            lax.fori_loop(i, KB, inner, 0)
            return 0
        lax.fori_loop(k + 1, KB, outer, 0)
        return 0

    lax.fori_loop(0, KB, step, 0)


VM = pl.BlockSpec(memory_space=pltpu.VMEM)
SM = pl.BlockSpec(memory_space=pltpu.SMEM)
PARAMS = pltpu.CompilerParams(vmem_limit_bytes=48 << 20)


def chol(packed, scale):
    return pl.pallas_call(
        lambda *refs: chol_kernel(scale, *refs),
        out_shape=(jax.ShapeDtypeStruct((N, N), F32), jax.ShapeDtypeStruct((N, NB), F32)),
        in_specs=[VM],
        out_specs=(VM, VM),
        scratch_shapes=[pltpu.VMEM((NB, 2 * NB), F32)],
        compiler_params=PARAMS,
        cost_estimate=pl.CostEstimate(flops=1 << 33, bytes_accessed=8 << 20, transcendentals=0),
        name="chol",
    )(packed)


def thin_kernel(core_ref, e_ref, ct_ref, rm_ref, ro_ref, wm_ref, wo_ref, ru_ref, ri_ref, out_ref, wu, wi, x, y):
    @pl.when(core_ref[0] == 0)
    def _():
        ru_ref[...] = rm_ref[...]
        ri_ref[...] = ro_ref[...]
        wu[...] = wm_ref[...]
        wi[...] = wo_ref[...]

    @pl.when(core_ref[0] != 0)
    def _():
        ru_ref[...] = ro_ref[...]
        ri_ref[...] = rm_ref[...]
        wu[...] = wo_ref[...]
        wi[...] = wm_ref[...]

    x[...] = e_ref[...]
    for k in range(KB - 1, -1, -1):
        lo, hi = k * NB, (k + 1) * NB
        xk = dot(x[:, lo:hi], wu[lo:hi, :], 1, 0)
        x[:, lo:hi] = xk
        if k:
            x[:, :lo] = x[:, :lo] - dot(xk, ru_ref[:lo, lo:hi], 1, 1)
    y[...] = dot(x[...], ct_ref[...], 1, 1)
    for k in range(KB):
        lo, hi = k * NB, (k + 1) * NB
        yk = dot(y[:, lo:hi], wi[lo:hi, :], 1, 1)
        out_ref[:, lo:hi] = yk
        if hi < N:
            y[:, hi:] = y[:, hi:] - dot(yk, ri_ref[lo:hi, hi:], 1, 0)


def thin(core, e, ct, rm, ro, wm, wo):
    full = jax.ShapeDtypeStruct((N, N), F32)
    return pl.pallas_call(
        thin_kernel,
        out_shape=(full, full, jax.ShapeDtypeStruct(e.shape, F32)),
        in_specs=[SM] + [VM] * 6,
        out_specs=(VM, VM, VM),
        scratch_shapes=[pltpu.VMEM((N, NB), F32)] * 2 + [pltpu.VMEM(e.shape, F32)] * 2,
        compiler_params=PARAMS,
        name="thin",
    )(core, e, ct, rm, ro, wm, wo)


def ring(k):
    return [(i, (i + k) % 4) for i in range(4)]


def shift(b, axis, k):
    return lax.ppermute(b, axis, ring(k % 4))


def swap(b):
    return lax.ppermute(b, "core", [(0, 1), (1, 0)])


def cut(b, at, dim):
    return lax.slice_in_dim(b, 0, at, axis=dim), lax.slice_in_dim(b, at, b.shape[dim], axis=dim)


def middle(b, dim):
    unit = NB if dim == -1 else 8
    dim = dim % b.ndim
    return b.shape[dim] // unit // 2 * unit, dim


def reduce4(b, axis, dim, split):
    i = lax.axis_index(axis)
    pick = lambda k: lax.dynamic_index_in_dim(b, (i + k) % 4, dim, keepdims=False)
    far = pick(2)
    at, sd = middle(far, split)
    fa, fb = cut(far, at, sd)
    fa, fb = shift(fa, axis, 1), shift(fb, axis, -1)
    na, nb = cut(pick(1), at, sd)
    pa, pb = cut(pick(3), at, sd)
    up = jnp.concatenate([na + fa, nb], sd)
    down = jnp.concatenate([pa, pb + fb], sd)
    return pick(0) + shift(up, axis, 1) + shift(down, axis, -1)


def gather4(b, axis, dim, split):
    i = lax.axis_index(axis)
    left, right = shift(b, axis, 1), shift(b, axis, -1)
    at, sd = middle(b, split)
    fa, fb = shift(cut(left, at, sd)[0], axis, 1), shift(cut(right, at, sd)[1], axis, -1)
    far = jnp.concatenate([fa, fb], sd)
    out = jnp.zeros(b.shape[:dim] + (4,) + b.shape[dim:], b.dtype)
    for k, part in ((0, b), (1, left), (2, far), (3, right)):
        out = lax.dynamic_update_index_in_dim(out, part, (i - k) % 4, dim)
    return out


def reduce_order(b, names, order, split):
    names = list(names)
    for axis in order:
        dim = names.index(axis)
        b = reduce4(b, axis, dim, split)
        names.pop(dim)
    return b


def pack(g):
    return jnp.concatenate([g[NB * i:NB * (i + 1), NB * j:NB * (j + 1)] for i, j in PAIRS_OF], 0)


def gram_dot(a, b):
    return lax.dot_general(a, b, (((0,), (0,)), ((), ())), preferred_element_type=F32)


def reduced_gram(user, item, core):
    keep = jnp.where(core == 0, user, item)
    give = jnp.where(core == 0, item, user)
    b = (keep + swap(give)).reshape(4, 4, 4, 72, NB)
    pa, pb = cut(b, 40, 3)
    pa = reduce_order(pa, ("y", "z", "x"), ("y", "z", "x"), -2)
    pb = reduce_order(pb, ("y", "z", "x"), ("z", "y", "x"), -2)
    pa, pb = gather4(pa, "x", 0, -2), gather4(pb, "x", 0, -2)
    pa = gather4(gather4(pa, "z", 0, -2), "y", 0, -2)
    pb = gather4(gather4(pb, "y", 0, -2), "z", 1, -2)
    return jnp.concatenate([pa, pb], 3).reshape(36 * NB, NB)


def reduced_cross(ct, core):
    b = ct.reshape(4, 4, 2, 4, 8, N)
    keep = lax.dynamic_index_in_dim(b, core, 2, keepdims=False)
    give = lax.dynamic_index_in_dim(b, 1 - core, 2, keepdims=False)
    b = keep + swap(give)
    parts = (b[..., :384], b[..., 384:768], b[..., 768:])
    orders = (("y", "z", "x"), ("z", "x", "y"), ("x", "y", "z"))
    return jnp.concatenate([reduce_order(p, ("y", "z", "x"), o, -1) for p, o in zip(parts, orders)], -1)


def slot_lists(pair_user, pair_item, pair_owner, pair_count, users, items):
    slots = pair_owner.shape[0]
    capacity = slots // 2
    keep = jnp.arange(slots, dtype=jnp.int32) < pair_count[0]
    owner = jnp.where(keep, pair_owner, -1)
    hot = (owner[None, :] == jnp.arange(4, dtype=jnp.int32)[:, None]).reshape(4, slots // NB, NB)
    tri = (jnp.arange(NB)[:, None] <= jnp.arange(NB)[None, :]).astype(BF16)
    inside = lax.dot_general(hot.astype(BF16), tri, (((2,), (0,)), ((), ())), preferred_element_type=F32)
    totals = inside[:, :, -1]
    before = jnp.cumsum(totals, axis=1) - totals
    rank = jnp.where(hot, inside + before[:, :, None] - 1.0, 0.0)
    place = jnp.sum(rank, axis=0).reshape(slots).astype(jnp.int32)
    flat = jnp.where(keep, owner * capacity + place, -1)
    code = pair_user * items + pair_item + 1
    spots = jnp.arange(4 * capacity, dtype=jnp.int32)
    return jnp.sum(jnp.where(flat[None, :] == spots[:, None], code[None, :], 0), axis=1).reshape(4, capacity)


def body(user_table, item_table, pair_user, pair_item, pair_owner, pair_count):
    users, width = user_table.shape
    items = item_table.shape[0]
    slots = pair_user.shape[0]
    total = float(slots * 128)
    core, x = lax.axis_index("core"), lax.axis_index("x")

    from_left, from_right = shift(user_table, "x", 1), shift(user_table, "x", -1)
    far_a = shift(from_left[:users // 2], "x", 1)
    far_b = shift(from_right[users // 2:], "x", -1)

    codes = slot_lists(pair_user, pair_item, pair_owner, pair_count, users, items)
    named = codes > 0
    want = jnp.stack([jnp.where(named, (codes - 1) // items, -1), jnp.where(named, (codes - 1) % items, 0)], 1)
    pick = lambda k: lax.dynamic_index_in_dim(want, (x + k) % 4, 0, keepdims=False)
    lists = [pick(0)] + [shift(pick(k), "x", k) for k in (1, 2, 3)]

    keep = jnp.arange(slots, dtype=jnp.int32) < pair_count[0]
    mine = jnp.where(keep, pair_user, -1)
    times = jnp.sum((mine[None, :] == jnp.arange(users, dtype=jnp.int32)[:, None]).astype(F32), axis=1)
    weighted = user_table.astype(F32) * times[:, None]
    high = lax.reduce_precision(weighted, 8, 7)
    low = weighted - high
    gram_user = gram_dot(jnp.concatenate([user_table, user_table], 0), jnp.concatenate([high.astype(BF16), low.astype(BF16)], 0))

    rows = jnp.concatenate([l[0] for l in lists], 0)
    cols = jnp.concatenate([l[1] for l in lists], 0)
    item_panel = jnp.take(item_table, cols, axis=0, mode="clip")
    item_panel = jnp.where((rows >= 0)[:, None], item_panel, jnp.zeros((), BF16))
    gram_item = gram_dot(item_panel, item_panel)
    packed = reduced_gram(pack(gram_user), pack(gram_item), core)

    def users_of(k, table):
        r = lists[k][0]
        got = jnp.take(table, jnp.maximum(r, 0), axis=0, mode="clip")
        return jnp.where((r >= 0)[:, None], got, jnp.zeros((), BF16))
    far = jnp.concatenate([far_a, far_b], 0)
    user_panel = jnp.concatenate([users_of(0, user_table), users_of(1, from_left), users_of(2, far), users_of(3, from_right)], 0)
    ct = reduced_cross(gram_dot(item_panel, user_panel), core)

    r_mine, w_mine = chol(packed, 1.0 / total)
    ct = lax.all_gather(ct, ALL, tiled=True)
    r_other, w_other = swap(r_mine), swap(w_mine)
    position = lax.axis_index(ALL)
    at = lax.broadcasted_iota(jnp.int32, (8, width), 0) + position * 8
    pick8 = (at == lax.broadcasted_iota(jnp.int32, (8, width), 1)).astype(F32)
    r_user, r_item, whitened = thin(core.reshape(1), pick8 * float(total) ** -0.5, ct, r_mine, r_other, w_mine, w_other)
    return (r_user, r_item, whitened)


def solution(mesh):
    fine = Mesh(mesh.devices.reshape(4, 4, 2, 4), ALL)
    placed = (P(ALL, None), P("x", None), P(ALL), P(ALL), P(ALL), P(ALL))
    return jax.shard_map(
        body,
        mesh=fine,
        in_specs=placed,
        out_specs=(P(), P(), P(ALL, None)),
        check_vma=False,
    )
```

```python
import functools

import jax
import jax.numpy as jnp
from jax import lax
from jax.experimental import pallas as pl
from jax.experimental.pallas import tpu as pltpu
from jax.sharding import Mesh, PartitionSpec as P

N = 1024
NB = 128
KB = N // NB
SUB = 32
HI = lax.Precision.HIGHEST
F32 = jnp.float32
BF16 = jnp.bfloat16
ALL = ("y", "z", "core", "x")
PAIRS_OF = [(i, j) for i in range(KB) for j in range(i, KB)]
START = {ij: NB * n for n, ij in enumerate(PAIRS_OF)}


def row_of(v, t):
    return jnp.broadcast_to(v[t:t + 1, :], v.shape)


def lane_of(v, c):
    return jnp.broadcast_to(v[:, c:c + 1], (8, NB))


def dot(a, b, ca, cb):
    return lax.dot_general(a, b, (((ca,), (cb,)), ((), ())), precision=HI, preferred_element_type=F32)


def factor(refs):
    sub = lax.broadcasted_iota(jnp.int32, (8, NB), 0)
    groups = SUB // 8
    for s in range(NB // SUB):
        panels = [[(r[SUB * s + 8 * g:SUB * s + 8 * g + 8, :NB], r[SUB * s + 8 * g:SUB * s + 8 * g + 8, NB:]) for g in range(groups)] for r in refs]
        for g in range(groups):
            for m, r in enumerate(refs):
                base = SUB * s + 8 * g
                left, right = panels[m][g]
                cols = [lane_of(left, base + t) for t in range(8)]
                fac = [[None] * 8 for _ in range(8)]
                inv = []
                rows_l, rows_r = [], []
                for t in range(8):
                    d = row_of(cols[t], t)
                    ri = lax.rsqrt(d)
                    inv.append(ri)
                    lt = cols[t] * ri
                    for u in range(t + 1, 8):
                        fac[t][u] = row_of(lt, u)
                        cols[u] = cols[u] - lt * fac[t][u]
                    pl_, pr_ = row_of(left, t), row_of(right, t)
                    for k in range(t):
                        pl_ = pl_ - fac[k][t] * rows_l[k]
                        pr_ = pr_ - fac[k][t] * rows_r[k]
                    rows_l.append(pl_ * ri)
                    rows_r.append(pr_ * ri)
                for h in range(g + 1, groups):
                    hl, hr = panels[m][h]
                    hc = [lane_of(hl, base + t) for t in range(8)]
                    for t in range(8):
                        ht = hc[t] * inv[t]
                        for u in range(t + 1, 8):
                            hc[u] = hc[u] - ht * fac[t][u]
                        hl = hl - ht * rows_l[t]
                        hr = hr - ht * rows_r[t]
                    panels[m][h] = (hl, hr)
                out_l, out_r = rows_l[0], rows_r[0]
                for t in range(1, 8):
                    out_l = jnp.where(sub == t, rows_l[t], out_l)
                    out_r = jnp.where(sub == t, rows_r[t], out_r)
                r[base:base + 8, :NB] = out_l
                r[base:base + 8, NB:] = out_r
        lo = SUB * (s + 1)
        if lo < NB:
            for r in refs:
                got = r[SUB * s:lo, :]
                r[lo:, :] = r[lo:, :] - dot(got[:, lo:NB], got, 0, 0)


def chol_kernel(scale, g_ref, r_ref, w_ref, a):
    row = lax.broadcasted_iota(jnp.int32, (NB, NB), 0)
    col = lax.broadcasted_iota(jnp.int32, (NB, NB), 1)
    eye = (row == col).astype(F32)
    for i in range(KB):
        if i:
            r_ref[NB * i:NB * (i + 1), :NB * i] = jnp.zeros((NB, NB * i), F32)
        for j in range(i, KB):
            at = START[i, j]
            r_ref[NB * i:NB * (i + 1), NB * j:NB * (j + 1)] = g_ref[at:at + NB, :] * scale

    def step(k, _):
        at = pl.multiple_of(k * NB, NB)
        here = pl.ds(at, NB)
        a[:, :NB] = r_ref[here, here]
        a[:, NB:] = eye
        factor([a])
        w_ref[here, :] = a[:, NB:]
        r_ref[here, here] = jnp.where(col >= row, a[:, :NB], 0.0)

        def panel(j, _):
            there = pl.ds(pl.multiple_of(j * NB, NB), NB)
            r_ref[here, there] = dot(a[:, NB:], r_ref[here, there], 1, 0)
            return 0
        lax.fori_loop(k + 1, KB, panel, 0)

        def outer(i, _):
            mine = pl.ds(pl.multiple_of(i * NB, NB), NB)

            def inner(j, _):
                there = pl.ds(pl.multiple_of(j * NB, NB), NB)
                r_ref[mine, there] = r_ref[mine, there] - dot(r_ref[here, mine], r_ref[here, there], 0, 0)
                return 0
            lax.fori_loop(i, KB, inner, 0)
            return 0
        lax.fori_loop(k + 1, KB, outer, 0)
        return 0

    lax.fori_loop(0, KB, step, 0)


VM = pl.BlockSpec(memory_space=pltpu.VMEM)
SM = pl.BlockSpec(memory_space=pltpu.SMEM)
PARAMS = pltpu.CompilerParams(vmem_limit_bytes=48 << 20)


def chol(packed, scale):
    return pl.pallas_call(
        lambda *refs: chol_kernel(scale, *refs),
        out_shape=(jax.ShapeDtypeStruct((N, N), F32), jax.ShapeDtypeStruct((N, NB), F32)),
        in_specs=[VM],
        out_specs=(VM, VM),
        scratch_shapes=[pltpu.VMEM((NB, 2 * NB), F32)],
        compiler_params=PARAMS,
        cost_estimate=pl.CostEstimate(flops=1 << 33, bytes_accessed=8 << 20, transcendentals=0),
        name="chol",
    )(packed)


def thin_kernel(core_ref, y_ref, rm_ref, ro_ref, wm_ref, wo_ref, r_ref, out_ref, w, y, sem, *, maker):
    @pl.when(core_ref[0] == maker)
    def _():
        copy = pltpu.make_async_copy(rm_ref, r_ref, sem)
        copy.start()
        w[...] = wm_ref[...]
        copy.wait()

    @pl.when(core_ref[0] != maker)
    def _():
        copy = pltpu.make_async_copy(ro_ref, r_ref, sem)
        copy.start()
        w[...] = wo_ref[...]
        copy.wait()

    y[...] = y_ref[...]
    for k in range(KB):
        lo, hi = k * NB, (k + 1) * NB
        yk = dot(y[:, lo:hi], w[lo:hi, :], 1, 1)
        out_ref[:, lo:hi] = yk
        if hi < N:
            y[:, hi:] = y[:, hi:] - dot(yk, r_ref[lo:hi, hi:], 1, 0)


def thin(core, y, rm, ro, wm, wo, maker):
    return pl.pallas_call(
        functools.partial(thin_kernel, maker=maker),
        out_shape=(jax.ShapeDtypeStruct((N, N), F32), jax.ShapeDtypeStruct(y.shape, F32)),
        in_specs=[SM, VM, pl.BlockSpec(memory_space=pl.ANY), pl.BlockSpec(memory_space=pl.ANY), VM, VM],
        out_specs=(VM, VM),
        scratch_shapes=[pltpu.VMEM((N, NB), F32), pltpu.VMEM(y.shape, F32), pltpu.SemaphoreType.DMA],
        compiler_params=PARAMS,
        name="thin",
    )(core, y, rm, ro, wm, wo)


CHIPS = ("y", "z", "x")
CORE_FIRST = ("core", "y", "z", "x")


def swap(b):
    return lax.ppermute(b, "core", [(0, 1), (1, 0)])


def pack(g):
    return jnp.concatenate([g[NB * i:NB * (i + 1), NB * j:NB * (j + 1)] for i, j in PAIRS_OF], 0)


def gram_dot(a, b):
    return lax.dot_general(a, b, (((0,), (0,)), ((), ())), preferred_element_type=F32)


def weighted_gram(table, times):
    weighted = table.astype(F32) * times[:, None]
    high = lax.reduce_precision(weighted, 8, 7)
    parts = jnp.concatenate([high.astype(BF16), (weighted - high).astype(BF16)], 0)
    return gram_dot(jnp.concatenate([table, table], 0), parts)


def histogram(key, bins):
    hot = (key[None, :] // NB == jnp.arange(bins // NB, dtype=jnp.int32)[:, None]) & (key >= 0)[None, :]
    lane = key[:, None] % NB == jnp.arange(NB, dtype=jnp.int32)[None, :]
    return lax.dot_general(hot.astype(BF16), lane.astype(BF16), (((1,), (0,)), ((), ())), preferred_element_type=F32)


def chip_scatter(b):
    return jnp.sum(lax.all_to_all(b, CHIPS, 0, 0, tiled=True), 0)


def chip_gather(b):
    return lax.all_to_all(jnp.broadcast_to(b[None], (64,) + b.shape), CHIPS, 0, 0, tiled=True)


def body(user_table, item_table, pair_user, pair_item, pair_owner, pair_count):
    users, width = user_table.shape
    items = item_table.shape[0]
    slots = pair_user.shape[0]
    total = float(slots * 128)
    core, x = lax.axis_index("core"), lax.axis_index("x")

    part = items // 32
    q = lax.axis_index(("y", "z", "core"))
    whole = lax.all_gather(lax.dynamic_slice_in_dim(item_table, q * part, part, 0), ALL, tiled=True)

    keep = jnp.arange(slots, dtype=jnp.int32) < pair_count[0]
    here = histogram(jnp.where(keep, pair_owner * items + pair_item, -1), 4 * items)
    named = jnp.sum(lax.all_to_all(here.reshape(4, items // NB, NB), "x", 0, 0, tiled=True), 0).reshape(items)
    gram_user = weighted_gram(user_table, histogram(jnp.where(keep, pair_user, -1), users).reshape(users))
    gram_item = weighted_gram(item_table, named)

    user, item = pack(gram_user), pack(gram_item)
    mine = jnp.where(core == 0, user, item) + swap(jnp.where(core == 0, item, user))
    packed = chip_gather(chip_scatter(mine.reshape(64, 72, NB))).reshape(36 * NB, NB)

    user_panel = jnp.where(keep[:, None], jnp.take(user_table, pair_user, axis=0, mode="clip"), jnp.zeros((), BF16))
    rows = (pair_item // part * 4 + pair_owner) * part + pair_item % part
    item_panel = jnp.where(keep[:, None], jnp.take(whole, rows, axis=0, mode="clip"), jnp.zeros((), BF16))
    ct = gram_dot(item_panel, user_panel).reshape(2, width // 2, width)
    half = lax.dynamic_index_in_dim(ct, core, 0, keepdims=False)
    half = half + swap(lax.dynamic_index_in_dim(ct, 1 - core, 0, keepdims=False))
    packed, half = lax.optimization_barrier((packed, half))
    ct = chip_scatter(half.reshape(64, 8, width))

    r_mine, w_mine = chol(packed, 1.0 / total)
    r_other, w_other = swap(r_mine), swap(w_mine)
    flag = core.reshape(1)
    r_user, left = thin(flag, ct * float(total) ** -0.5, r_mine, r_other, w_mine, w_other, 0)
    left = left.reshape(8, 4, 4, 2, 4, 8).transpose(3, 1, 2, 4, 0, 5).reshape(128, 64)
    left = lax.all_to_all(left, CORE_FIRST, 0, 0, tiled=True)
    left = left.reshape(width, 8).T
    r_item, whitened = thin(flag, left, r_mine, r_other, w_mine, w_other, 1)
    return (r_user, r_item, whitened)


def solution(mesh):
    fine = Mesh(mesh.devices.reshape(4, 4, 2, 4), ALL)
    placed = (P(ALL, None), P("x", None), P(ALL), P(ALL), P(ALL), P(ALL))
    return jax.shard_map(
        body,
        mesh=fine,
        in_specs=placed,
        out_specs=(P(), P(), P(ALL, None)),
        check_vma=False,
    )
```

```python
import functools

import jax
import jax.numpy as jnp
from jax import lax
from jax.experimental import pallas as pl
from jax.experimental.pallas import tpu as pltpu
from jax.sharding import Mesh, PartitionSpec as P


N = 1024
NB = 128
KB = N // NB
SUB = 32
CHUNK = 512
HI = lax.Precision.HIGHEST
F32 = jnp.float32
BF16 = jnp.bfloat16
ALL = ("y", "z", "core", "x")
PAIRS_OF = [(i, j) for i in range(KB) for j in range(i, KB)]
START = {ij: NB * n for n, ij in enumerate(PAIRS_OF)}


def row_of(v, t):
    return jnp.broadcast_to(v[t:t + 1, :], v.shape)


def lane_of(v, c):
    return jnp.broadcast_to(v[:, c:c + 1], (8, NB))


def dot(a, b, ca, cb):
    return lax.dot_general(a, b, (((ca,), (cb,)), ((), ())), precision=HI, preferred_element_type=F32)


def parts(a):
    h = a.astype(BF16)
    rest = a - h.astype(F32)
    m = rest.astype(BF16)
    return h, m, (rest - m.astype(F32)).astype(BF16)


def stacks(a):
    h, m, l = parts(a)
    return jnp.concatenate([h, h, m, m, h, l], 0), jnp.concatenate([h, m, h, m, l, h], 0)


def tdot(a, b):
    return lax.dot_general(a, b, (((0,), (0,)), ((), ())), preferred_element_type=F32)


def factor(a):
    sub = lax.broadcasted_iota(jnp.int32, (8, NB), 0)
    groups = SUB // 8
    for s in range(NB // SUB):
        lo = SUB * s
        left = [a[lo + 8 * g:lo + 8 * g + 8, :NB] for g in range(groups)]
        right = [a[lo + 8 * g:lo + 8 * g + 8, NB:] for g in range(groups)]
        for g in range(groups):
            base = lo + 8 * g
            cols = [lane_of(left[g], base + t) for t in range(8)]
            ent = {(u, t): row_of(cols[t], u) for t in range(8) for u in range(t, 8)}
            fac, inv = {}, []
            for t in range(8):
                ri = lax.rsqrt(ent[t, t])
                inv.append(ri)
                for u in range(t + 1, 8):
                    fac[t, u] = ent[u, t] * ri
                for v in range(t + 1, 8):
                    for u in range(v, 8):
                        ent[u, v] = ent[u, v] - fac[t, u] * fac[t, v]
            rows_l, rows_r = [], []
            for t in range(8):
                pl_, pr_ = row_of(left[g], t), row_of(right[g], t)
                for k in range(t):
                    pl_ = pl_ - fac[k, t] * rows_l[k]
                    pr_ = pr_ - fac[k, t] * rows_r[k]
                rows_l.append(pl_ * inv[t])
                rows_r.append(pr_ * inv[t])
            for h in range(g + 1, groups):
                hc = [lane_of(left[h], base + t) for t in range(8)]
                for t in range(8):
                    ht = hc[t] * inv[t]
                    for u in range(t + 1, 8):
                        hc[u] = hc[u] - ht * fac[t, u]
                    left[h] = left[h] - ht * rows_l[t]
                    right[h] = right[h] - ht * rows_r[t]
            out_l, out_r = rows_l[0], rows_r[0]
            for t in range(1, 8):
                out_l = jnp.where(sub == t, rows_l[t], out_l)
                out_r = jnp.where(sub == t, rows_r[t], out_r)
            a[base:base + 8, :NB] = out_l
            a[base:base + 8, NB:] = out_r
        hi = lo + SUB
        if hi < NB:
            got = a[lo:hi, :]
            sa, sb = stacks(got)
            a[hi:, :] = a[hi:, :] - tdot(sa[:, hi:NB], sb)


def chol_kernel(scale, g_ref, r_ref, w_ref, a):
    row = lax.broadcasted_iota(jnp.int32, (NB, NB), 0)
    col = lax.broadcasted_iota(jnp.int32, (NB, NB), 1)
    eye = (row == col).astype(F32)
    for i in range(KB):
        for j in range(i, KB):
            at = START[i, j]
            r_ref[NB * i:NB * (i + 1), NB * j:NB * (j + 1)] = g_ref[at:at + NB, :] * scale

    def step(k, _):
        here = pl.ds(pl.multiple_of(k * NB, NB), NB)
        a[:, :NB] = r_ref[here, here]
        a[:, NB:] = eye
        factor(a)
        w_ref[here, :] = a[:, NB:]
        r_ref[here, here] = jnp.where(col >= row, a[:, :NB], 0.0)
        for s in range(KB - 1):
            @pl.when(k == s)
            def _(s=s):
                lo = NB * (s + 1)
                panel = dot(a[:, NB:], r_ref[NB * s:lo, lo:], 1, 0)
                r_ref[NB * s:lo, lo:] = panel
                sa, sb = stacks(panel)
                for i in range(lo, N, 256):
                    n = min(256, N - i)
                    r_ref[i:i + n, i:] = r_ref[i:i + n, i:] - tdot(sa[:, i - lo:i - lo + n], sb[:, i - lo:])
        return 0

    lax.fori_loop(0, KB, step, 0)
    for i in range(1, KB):
        r_ref[NB * i:NB * (i + 1), :NB * i] = jnp.zeros((NB, NB * i), F32)


VM = pl.BlockSpec(memory_space=pltpu.VMEM)
HBM = pl.BlockSpec(memory_space=pltpu.HBM)
SM = pl.BlockSpec(memory_space=pltpu.SMEM)
PARAMS = pltpu.CompilerParams(vmem_limit_bytes=48 << 20)


def chol(packed, scale):
    return pl.pallas_call(
        functools.partial(chol_kernel, scale),
        out_shape=(jax.ShapeDtypeStruct((N, N), F32), jax.ShapeDtypeStruct((N, NB), F32)),
        in_specs=[VM],
        out_specs=(VM, VM),
        scratch_shapes=[pltpu.VMEM((NB, 2 * NB), F32)],
        compiler_params=PARAMS,
        cost_estimate=pl.CostEstimate(flops=1 << 33, bytes_accessed=8 << 20, transcendentals=0),
        name="chol",
    )(packed)


def thin_kernel(core_ref, y_ref, rm_ref, ro_ref, wm_ref, wo_ref, r_ref, out_ref, r, w, y, sem, *, maker):
    def load(r_from, w_from):
        copy = pltpu.make_async_copy(r_from, r, sem)
        copy.start()
        w[...] = w_from[...]
        copy.wait()

    pl.when(core_ref[0] == maker)(lambda: load(rm_ref, wm_ref))
    pl.when(core_ref[0] != maker)(lambda: load(ro_ref, wo_ref))
    keep = pltpu.make_async_copy(r, r_ref, sem)
    keep.start()
    y[...] = y_ref[...]
    for k in range(KB):
        lo, hi = k * NB, (k + 1) * NB
        yk = dot(y[:, lo:hi], w[lo:hi, :], 1, 1)
        out_ref[:, lo:hi] = yk
        if hi < N:
            y[:, hi:] = y[:, hi:] - dot(yk, r[lo:hi, hi:], 1, 0)
    keep.wait()


def thin(core, y, rm, ro, wm, wo, maker):
    return pl.pallas_call(
        functools.partial(thin_kernel, maker=maker),
        out_shape=(jax.ShapeDtypeStruct((N, N), F32), jax.ShapeDtypeStruct(y.shape, F32)),
        in_specs=[SM, VM, HBM, HBM, VM, VM],
        out_specs=(HBM, VM),
        scratch_shapes=[pltpu.VMEM((N, N), F32), pltpu.VMEM((N, NB), F32), pltpu.VMEM(y.shape, F32), pltpu.SemaphoreType.DMA],
        compiler_params=PARAMS,
        name="thin",
    )(core, y, rm, ro, wm, wo)


def gram_kernel(core_ref, cu_ref, ci_ref, u_ref, i_ref, keep_ref, give_ref, counts, acc):
    eye = lax.broadcasted_iota(jnp.int32, (NB, NB), 0) == lax.broadcasted_iota(jnp.int32, (NB, NB), 1)

    def put(ref):
        for i, j in PAIRS_OF:
            at = START[i, j]
            ref[at:at + NB, :] = acc[NB * i:NB * (i + 1), NB * j:NB * (j + 1)]

    for maker, table in enumerate((u_ref, i_ref)):
        rows = table.shape[0]
        counts[:rows // NB, :] = ci_ref[0] + ci_ref[1] + ci_ref[2] + ci_ref[3] if maker else cu_ref[...]
        for c in range(rows // CHUNK):
            blocks = range(c * (CHUNK // NB), (c + 1) * (CHUNK // NB))
            times = jnp.concatenate([jnp.sum(jnp.where(eye, counts[b:b + 1, :], 0.0), axis=1, keepdims=True) for b in blocks], 0)
            t = table[c * CHUNK:(c + 1) * CHUNK, :]
            weighted = t.astype(F32) * times
            high = weighted.astype(BF16)
            both = jnp.concatenate([high, (weighted - high.astype(F32)).astype(BF16)], 0)
            tt = jnp.concatenate([t, t], 0)
            for i in range(0, N, 256):
                got = tdot(tt[:, i:i + 256], both[:, i:])
                acc[i:i + 256, i:] = acc[i:i + 256, i:] + got if c else got
        pl.when(core_ref[0] == maker)(lambda: put(keep_ref))
        pl.when(core_ref[0] != maker)(lambda: put(give_ref))


def grams(core, user_counts, item_counts, user_table, item_table):
    packed = jax.ShapeDtypeStruct((36 * NB, NB), F32)
    return pl.pallas_call(
        gram_kernel,
        out_shape=(packed, packed),
        in_specs=[SM, VM, VM, VM, VM],
        out_specs=(VM, VM),
        scratch_shapes=[pltpu.VMEM((16, NB), F32), pltpu.VMEM((N, N), F32)],
        compiler_params=PARAMS,
        cost_estimate=pl.CostEstimate(flops=1 << 33, bytes_accessed=10 << 20, transcendentals=0),
        name="grams",
    )(core, user_counts, item_counts, user_table, item_table)


CHIPS = ("y", "z", "x")
CORE_FIRST = ("core", "y", "z", "x")


def swap(b):
    return lax.ppermute(b, "core", [(0, 1), (1, 0)])


def gram_dot(a, b):
    return lax.dot_general(a, b, (((0,), (0,)), ((), ())), preferred_element_type=F32)


def histogram(key, bins):
    hot = (key[None, :] // NB == jnp.arange(bins // NB, dtype=jnp.int32)[:, None]) & (key >= 0)[None, :]
    lane = key[:, None] % NB == jnp.arange(NB, dtype=jnp.int32)[None, :]
    return lax.dot_general(hot.astype(BF16), lane.astype(BF16), (((1,), (0,)), ((), ())), preferred_element_type=F32)


def chip_scatter(b):
    return jnp.sum(lax.all_to_all(b, CHIPS, 0, 0, tiled=True), 0)


def chip_gather(b):
    return lax.all_to_all(jnp.broadcast_to(b[None], (64,) + b.shape), CHIPS, 0, 0, tiled=True)


def body(user_table, item_table, pair_user, pair_item, pair_owner, pair_count):
    users, width = user_table.shape
    items = item_table.shape[0]
    slots = pair_user.shape[0]
    total = float(slots * 128)
    core = lax.axis_index("core")

    part = items // 32
    q = lax.axis_index(("y", "z", "core"))
    whole = lax.all_gather(lax.dynamic_slice_in_dim(item_table, q * part, part, 0), ALL, tiled=True)

    keep = jnp.arange(slots, dtype=jnp.int32) < pair_count[0]
    here = histogram(jnp.where(keep, pair_owner * items + pair_item, -1), 4 * items)
    flag = core.reshape(1)
    named = lax.all_to_all(here.reshape(4, items // NB, NB), "x", 0, 0, tiled=True)
    keep_half, give_half = grams(flag, histogram(jnp.where(keep, pair_user, -1), users), named, user_table, item_table)
    mine = keep_half + swap(give_half)
    mine = chip_scatter(mine.reshape(64, 72, NB))
    packed = chip_gather(mine).reshape(36 * NB, NB)

    user_panel = jnp.where(keep[:, None], jnp.take(user_table, pair_user, axis=0, mode="clip"), jnp.zeros((), BF16))
    rows = (pair_item // part * 4 + pair_owner) * part + pair_item % part
    item_panel = jnp.where(keep[:, None], jnp.take(whole, rows, axis=0, mode="clip"), jnp.zeros((), BF16))
    ct = gram_dot(item_panel, user_panel).reshape(2, width // 2, width)
    half = lax.dynamic_index_in_dim(ct, core, 0, keepdims=False)
    half = half + swap(lax.dynamic_index_in_dim(ct, 1 - core, 0, keepdims=False))
    ct = chip_scatter(half.reshape(64, 8, width))

    r_mine, w_mine = chol(packed, 1.0 / total)
    r_other, w_other = swap(r_mine), swap(w_mine)
    r_user, left = thin(flag, ct * float(total) ** -0.5, r_mine, r_other, w_mine, w_other, 0)
    left = left.reshape(8, 4, 4, 2, 4, 8).transpose(3, 1, 2, 4, 0, 5).reshape(128, 64)
    left = lax.all_to_all(left, CORE_FIRST, 0, 0, tiled=True)
    left = left.reshape(width, 8).T
    r_item, whitened = thin(flag, left, r_mine, r_other, w_mine, w_other, 1)
    return (r_user, r_item, whitened)


def solution(mesh):
    fine = Mesh(mesh.devices.reshape(4, 4, 2, 4), ALL)
    placed = (P(ALL, None), P("x", None), P(ALL), P(ALL), P(ALL), P(ALL))

    return jax.shard_map(
        body,
        mesh=fine,
        in_specs=placed,
        out_specs=(P(), P(), P(ALL, None)),
        check_vma=False,
    )
```

```python
import functools

import jax
import jax.numpy as jnp
from jax import lax
from jax.experimental import pallas as pl
from jax.experimental.pallas import tpu as pltpu
from jax.sharding import Mesh, PartitionSpec as P


N = 1024
NB = 128
KB = N // NB
SUB = 32
CHUNK = 512
HI = lax.Precision.HIGHEST
F32 = jnp.float32
BF16 = jnp.bfloat16
ALL = ("y", "z", "core", "x")
PAIRS_OF = [(i, j) for i in range(KB) for j in range(i, KB)]
START = {ij: NB * n for n, ij in enumerate(PAIRS_OF)}


def row_of(v, t):
    return jnp.broadcast_to(v[t:t + 1, :], v.shape)


def lane_of(v, c):
    return jnp.broadcast_to(v[:, c:c + 1], (8, NB))


def dot(a, b, ca, cb):
    return lax.dot_general(a, b, (((ca,), (cb,)), ((), ())), precision=HI, preferred_element_type=F32)


def parts(a):
    h = a.astype(BF16)
    rest = a - h.astype(F32)
    m = rest.astype(BF16)
    return h, m, (rest - m.astype(F32)).astype(BF16)


def stacks(a):
    h, m, l = parts(a)
    return jnp.concatenate([h, h, m, m, h, l], 0), jnp.concatenate([h, m, h, m, l, h], 0)


def tdot(a, b):
    return lax.dot_general(a, b, (((0,), (0,)), ((), ())), preferred_element_type=F32)


def factor(a):
    sub = lax.broadcasted_iota(jnp.int32, (8, NB), 0)
    groups = SUB // 8
    for s in range(NB // SUB):
        lo = SUB * s
        left = [a[lo + 8 * g:lo + 8 * g + 8, :NB] for g in range(groups)]
        right = [a[lo + 8 * g:lo + 8 * g + 8, NB:] for g in range(groups)]
        for g in range(groups):
            base = lo + 8 * g
            cols = [lane_of(left[g], base + t) for t in range(8)]
            ent = {(u, t): row_of(cols[t], u) for t in range(8) for u in range(t, 8)}
            fac, inv = {}, []
            for t in range(8):
                ri = lax.rsqrt(ent[t, t])
                inv.append(ri)
                for u in range(t + 1, 8):
                    fac[t, u] = ent[u, t] * ri
                for v in range(t + 1, 8):
                    for u in range(v, 8):
                        ent[u, v] = ent[u, v] - fac[t, u] * fac[t, v]
            rows_l, rows_r = [], []
            for t in range(8):
                pl_, pr_ = row_of(left[g], t), row_of(right[g], t)
                for k in range(t):
                    pl_ = pl_ - fac[k, t] * rows_l[k]
                    pr_ = pr_ - fac[k, t] * rows_r[k]
                rows_l.append(pl_ * inv[t])
                rows_r.append(pr_ * inv[t])
            for h in range(g + 1, groups):
                hc = [lane_of(left[h], base + t) for t in range(8)]
                for t in range(8):
                    ht = hc[t] * inv[t]
                    for u in range(t + 1, 8):
                        hc[u] = hc[u] - ht * fac[t, u]
                    left[h] = left[h] - ht * rows_l[t]
                    right[h] = right[h] - ht * rows_r[t]
            out_l, out_r = rows_l[0], rows_r[0]
            for t in range(1, 8):
                out_l = jnp.where(sub == t, rows_l[t], out_l)
                out_r = jnp.where(sub == t, rows_r[t], out_r)
            a[base:base + 8, :NB] = out_l
            a[base:base + 8, NB:] = out_r
        hi = lo + SUB
        if hi < NB:
            got = a[lo:hi, :]
            sa, sb = stacks(got)
            a[hi:, :] = a[hi:, :] - tdot(sa[:, hi:NB], sb)


def chol_kernel(scale, g_ref, r_ref, w_ref, a):
    row = lax.broadcasted_iota(jnp.int32, (NB, NB), 0)
    col = lax.broadcasted_iota(jnp.int32, (NB, NB), 1)
    eye = (row == col).astype(F32)
    for i in range(KB):
        for j in range(i, KB):
            at = START[i, j]
            r_ref[NB * i:NB * (i + 1), NB * j:NB * (j + 1)] = g_ref[at:at + NB, :] * scale

    def step(k, _):
        here = pl.ds(pl.multiple_of(k * NB, NB), NB)
        a[:, :NB] = r_ref[here, here]
        a[:, NB:] = eye
        factor(a)
        w_ref[here, :] = a[:, NB:]
        r_ref[here, here] = jnp.where(col >= row, a[:, :NB], 0.0)
        for s in range(KB - 1):
            @pl.when(k == s)
            def _(s=s):
                lo = NB * (s + 1)
                panel = dot(a[:, NB:], r_ref[NB * s:lo, lo:], 1, 0)
                r_ref[NB * s:lo, lo:] = panel
                sa, sb = stacks(panel)
                for i in range(lo, N, 256):
                    n = min(256, N - i)
                    r_ref[i:i + n, i:] = r_ref[i:i + n, i:] - tdot(sa[:, i - lo:i - lo + n], sb[:, i - lo:])
        return 0

    lax.fori_loop(0, KB, step, 0)
    for i in range(1, KB):
        r_ref[NB * i:NB * (i + 1), :NB * i] = jnp.zeros((NB, NB * i), F32)


VM = pl.BlockSpec(memory_space=pltpu.VMEM)
HBM = pl.BlockSpec(memory_space=pltpu.HBM)
SM = pl.BlockSpec(memory_space=pltpu.SMEM)
PARAMS = pltpu.CompilerParams(vmem_limit_bytes=48 << 20)


def chol(packed, scale):
    return pl.pallas_call(
        functools.partial(chol_kernel, scale),
        out_shape=(jax.ShapeDtypeStruct((N, N), F32), jax.ShapeDtypeStruct((N, NB), F32)),
        in_specs=[VM],
        out_specs=(VM, VM),
        scratch_shapes=[pltpu.VMEM((NB, 2 * NB), F32)],
        compiler_params=PARAMS,
        cost_estimate=pl.CostEstimate(flops=1 << 33, bytes_accessed=8 << 20, transcendentals=0),
        name="chol",
    )(packed)


def thin_kernel(core_ref, y_ref, rm_ref, ro_ref, wm_ref, wo_ref, r_ref, out_ref, r, w, y, sem, *, maker):
    def load(r_from, w_from):
        copy = pltpu.make_async_copy(r_from, r, sem)
        copy.start()
        w[...] = w_from[...]
        copy.wait()

    pl.when(core_ref[0] == maker)(lambda: load(rm_ref, wm_ref))
    pl.when(core_ref[0] != maker)(lambda: load(ro_ref, wo_ref))
    keep = pltpu.make_async_copy(r, r_ref, sem)
    keep.start()
    y[...] = y_ref[...]
    for k in range(KB):
        lo, hi = k * NB, (k + 1) * NB
        yk = dot(y[:, lo:hi], w[lo:hi, :], 1, 1)
        out_ref[:, lo:hi] = yk
        if hi < N:
            y[:, hi:] = y[:, hi:] - dot(yk, r[lo:hi, hi:], 1, 0)
    keep.wait()


def thin(core, y, rm, ro, wm, wo, maker):
    return pl.pallas_call(
        functools.partial(thin_kernel, maker=maker),
        out_shape=(jax.ShapeDtypeStruct((N, N), F32), jax.ShapeDtypeStruct(y.shape, F32)),
        in_specs=[SM, VM, HBM, HBM, VM, VM],
        out_specs=(HBM, VM),
        scratch_shapes=[pltpu.VMEM((N, N), F32), pltpu.VMEM((N, NB), F32), pltpu.VMEM(y.shape, F32), pltpu.SemaphoreType.DMA],
        compiler_params=pltpu.CompilerParams(vmem_limit_bytes=60 << 20),
        name="thin",
    )(core, y, rm, ro, wm, wo)


def gram_kernel(core_ref, cu_ref, ci_ref, u_ref, i_ref, keep_ref, give_ref, counts, acc):
    eye = lax.broadcasted_iota(jnp.int32, (NB, NB), 0) == lax.broadcasted_iota(jnp.int32, (NB, NB), 1)

    def put(ref):
        for i, j in PAIRS_OF:
            at = START[i, j]
            ref[at:at + NB, :] = acc[NB * i:NB * (i + 1), NB * j:NB * (j + 1)]

    for maker, table in enumerate((u_ref, i_ref)):
        rows = table.shape[0]
        counts[:rows // NB, :] = ci_ref[...] if maker else cu_ref[...]
        for c in range(rows // CHUNK):
            blocks = range(c * (CHUNK // NB), (c + 1) * (CHUNK // NB))
            times = jnp.concatenate([jnp.sum(jnp.where(eye, counts[b:b + 1, :], 0.0), axis=1, keepdims=True) for b in blocks], 0)
            t = table[c * CHUNK:(c + 1) * CHUNK, :]
            weighted = t.astype(F32) * times
            high = weighted.astype(BF16)
            both = jnp.concatenate([high, (weighted - high.astype(F32)).astype(BF16)], 0)
            tt = jnp.concatenate([t, t], 0)
            for i in range(0, N, 256):
                got = tdot(tt[:, i:i + 256], both[:, i:])
                acc[i:i + 256, i:] = acc[i:i + 256, i:] + got if c else got
        pl.when(core_ref[0] == maker)(lambda: put(keep_ref))
        pl.when(core_ref[0] != maker)(lambda: put(give_ref))


def grams(core, user_counts, item_counts, user_table, item_table):
    packed = jax.ShapeDtypeStruct((36 * NB, NB), F32)
    return pl.pallas_call(
        gram_kernel,
        out_shape=(packed, packed),
        in_specs=[SM, VM, VM, VM, VM],
        out_specs=(VM, VM),
        scratch_shapes=[pltpu.VMEM((16, NB), F32), pltpu.VMEM((N, N), F32)],
        compiler_params=PARAMS,
        cost_estimate=pl.CostEstimate(flops=1 << 33, bytes_accessed=10 << 20, transcendentals=0),
        name="grams",
    )(core, user_counts, item_counts, user_table, item_table)


CHIPS = ("y", "z", "x")
CORE_FIRST = ("core", "y", "z", "x")


def swap(b):
    return lax.ppermute(b, "core", [(0, 1), (1, 0)])


def gram_dot(a, b):
    return lax.dot_general(a, b, (((0,), (0,)), ((), ())), preferred_element_type=F32)


def histogram(key, bins):
    hot = (key[None, :] // NB == jnp.arange(bins // NB, dtype=jnp.int32)[:, None]) & (key >= 0)[None, :]
    lane = key[:, None] % NB == jnp.arange(NB, dtype=jnp.int32)[None, :]
    return lax.dot_general(hot.astype(BF16), lane.astype(BF16), (((1,), (0,)), ((), ())), preferred_element_type=F32)


def chip_scatter(b):
    return jnp.sum(lax.all_to_all(b, CHIPS, 0, 0, tiled=True), 0)


def chip_gather(b):
    return lax.all_to_all(jnp.broadcast_to(b[None], (64,) + b.shape), CHIPS, 0, 0, tiled=True)


def ring(k):
    return [(i, (i + k) % 4) for i in range(4)]


def shift(b, axis, k):
    return lax.ppermute(b, axis, ring(k % 4))


def slot_lists(pair_user, pair_item, pair_owner, pair_count, items):
    slots = pair_owner.shape[0]
    capacity = slots // 2
    keep = jnp.arange(slots, dtype=jnp.int32) < pair_count[0]
    owner = jnp.where(keep, pair_owner, -1)
    hot = (owner[None, :] == jnp.arange(4, dtype=jnp.int32)[:, None]).reshape(4, slots // NB, NB)
    tri = (jnp.arange(NB)[:, None] <= jnp.arange(NB)[None, :]).astype(BF16)
    inside = lax.dot_general(hot.astype(BF16), tri, (((2,), (0,)), ((), ())), preferred_element_type=F32)
    totals = inside[:, :, -1]
    before = jnp.cumsum(totals, axis=1) - totals
    rank = jnp.where(hot, inside + before[:, :, None] - 1.0, 0.0)
    place = jnp.sum(rank, axis=0).reshape(slots).astype(jnp.int32)
    flat = jnp.where(keep, owner * capacity + place, -1)
    code = pair_user * items + pair_item + 1
    spots = jnp.arange(4 * capacity, dtype=jnp.int32)
    return jnp.sum(jnp.where(flat[None, :] == spots[:, None], code[None, :], 0), axis=1).reshape(4, capacity)


def body(user_table, item_table, pair_user, pair_item, pair_owner, pair_count):
    users, width = user_table.shape
    items = item_table.shape[0]
    slots = pair_user.shape[0]
    total = float(slots * 128)
    core, x = lax.axis_index("core"), lax.axis_index("x")
    flag = core.reshape(1)

    codes = slot_lists(pair_user, pair_item, pair_owner, pair_count, items)
    named = codes > 0
    want = jnp.stack([jnp.where(named, (codes - 1) // items, -1), jnp.where(named, (codes - 1) % items, 0)], 1)
    got = lax.all_to_all(want, "x", 0, 0, tiled=True)
    lists = jnp.concatenate([lax.dynamic_slice_in_dim(got, (x + k) % 4, 1, 0) for k in (0, 3, 1, 2)], 0)
    rows, cols = lists[:, 0].reshape(-1), lists[:, 1].reshape(-1)

    user_table_sent, want = lax.optimization_barrier((user_table, want))
    left, right = shift(user_table_sent, "x", 1), shift(user_table_sent, "x", -1)
    far_a, far_b = shift(left[:users // 2], "x", 1), shift(right[users // 2:], "x", -1)

    keep = jnp.arange(slots, dtype=jnp.int32) < pair_count[0]
    user_counts = histogram(jnp.where(keep, pair_user, -1), users)
    item_counts = histogram(jnp.where(rows >= 0, cols, -1), items)
    keep_half, give_half = grams(flag, user_counts, item_counts, user_table, item_table)
    mine = keep_half + swap(give_half)
    mine = chip_scatter(mine.reshape(64, 72, NB))
    packed = chip_gather(mine).reshape(36 * NB, NB)

    near = 3 * codes.shape[1]
    at = jnp.maximum(rows, 0).reshape(4, -1)
    item_panel = jnp.take(item_table, cols, axis=0, mode="clip")
    own_rows = jnp.take(user_table, at[0], axis=0, mode="clip")
    side_rows = [jnp.take(left, at[1], axis=0, mode="clip"), jnp.take(right, at[2], axis=0, mode="clip")]
    full = (rows >= 0)[:, None]
    masked = lambda a, b: jnp.where(full[a:b], item_panel[a:b], jnp.zeros((), BF16))
    ct = gram_dot(masked(0, near), jnp.concatenate([own_rows] + side_rows, 0))
    ct, far_a, far_b = lax.optimization_barrier((ct, far_a, far_b))
    far = jnp.take(jnp.concatenate([far_a, far_b], 0), at[3], axis=0, mode="clip")
    ct = ct + gram_dot(masked(near, rows.shape[0]), far)
    ct = ct.reshape(2, width // 2, width)
    half = lax.dynamic_index_in_dim(ct, core, 0, keepdims=False)
    half = half + swap(lax.dynamic_index_in_dim(ct, 1 - core, 0, keepdims=False))
    ct = chip_scatter(half.reshape(64, 8, width))

    r_mine, w_mine = chol(packed, 1.0 / total)
    r_other, w_other = swap(r_mine), swap(w_mine)
    r_user, left = thin(flag, ct * float(total) ** -0.5, r_mine, r_other, w_mine, w_other, 0)
    left = left.reshape(8, 4, 4, 2, 4, 8).transpose(3, 1, 2, 4, 0, 5).reshape(128, 64)
    left = lax.all_to_all(left, CORE_FIRST, 0, 0, tiled=True)
    left = left.reshape(width, 8).T
    r_item, whitened = thin(flag, left, r_mine, r_other, w_mine, w_other, 1)
    return (r_user, r_item, whitened)


def solution(mesh):
    fine = Mesh(mesh.devices.reshape(4, 4, 2, 4), ALL)
    placed = (P(ALL, None), P("x", None), P(ALL), P(ALL), P(ALL), P(ALL))

    return jax.shard_map(
        body,
        mesh=fine,
        in_specs=placed,
        out_specs=(P(), P(), P(ALL, None)),
        check_vma=False,
    )
```

```python
import functools

import jax
import jax.numpy as jnp
from jax import lax
from jax.experimental import pallas as pl
from jax.experimental.pallas import tpu as pltpu
from jax.sharding import Mesh, PartitionSpec as P


N = 1024
NB = 128
KB = N // NB
SUB = 32
CHUNK = 512
SLOTS = 1024
HI = lax.Precision.HIGHEST
F32 = jnp.float32
BF16 = jnp.bfloat16
ALL = ("y", "z", "core", "x")
PAIRS_OF = [(i, j) for i in range(KB) for j in range(i, KB)]
START = {ij: NB * n for n, ij in enumerate(PAIRS_OF)}


def row_of(v, t):
    return jnp.broadcast_to(v[t:t + 1, :], v.shape)


def lane_of(v, c):
    return jnp.broadcast_to(v[:, c:c + 1], (8, NB))


def dot(a, b, ca, cb):
    return lax.dot_general(a, b, (((ca,), (cb,)), ((), ())), precision=HI, preferred_element_type=F32)


def parts(a):
    h = a.astype(BF16)
    rest = a - h.astype(F32)
    m = rest.astype(BF16)
    return h, m, (rest - m.astype(F32)).astype(BF16)


def stacks(a):
    h, m, l = parts(a)
    return jnp.concatenate([h, h, m, m, h, l], 0), jnp.concatenate([h, m, h, m, l, h], 0)


def tdot(a, b):
    return lax.dot_general(a, b, (((0,), (0,)), ((), ())), preferred_element_type=F32)


def factor(a):
    sub = lax.broadcasted_iota(jnp.int32, (8, NB), 0)
    groups = SUB // 8
    for s in range(NB // SUB):
        lo = SUB * s
        left = [a[lo + 8 * g:lo + 8 * g + 8, :NB] for g in range(groups)]
        right = [a[lo + 8 * g:lo + 8 * g + 8, NB:] for g in range(groups)]
        for g in range(groups):
            base = lo + 8 * g
            cols = [lane_of(left[g], base + t) for t in range(8)]
            ent = {(u, t): row_of(cols[t], u) for t in range(8) for u in range(t, 8)}
            fac, inv = {}, []
            for t in range(8):
                ri = lax.rsqrt(ent[t, t])
                inv.append(ri)
                for u in range(t + 1, 8):
                    fac[t, u] = ent[u, t] * ri
                for v in range(t + 1, 8):
                    for u in range(v, 8):
                        ent[u, v] = ent[u, v] - fac[t, u] * fac[t, v]
            rows_l, rows_r = [], []
            for t in range(8):
                pl_, pr_ = row_of(left[g], t), row_of(right[g], t)
                for k in range(t):
                    pl_ = pl_ - fac[k, t] * rows_l[k]
                    pr_ = pr_ - fac[k, t] * rows_r[k]
                rows_l.append(pl_ * inv[t])
                rows_r.append(pr_ * inv[t])
            for h in range(g + 1, groups):
                hc = [lane_of(left[h], base + t) for t in range(8)]
                for t in range(8):
                    ht = hc[t] * inv[t]
                    for u in range(t + 1, 8):
                        hc[u] = hc[u] - ht * fac[t, u]
                    left[h] = left[h] - ht * rows_l[t]
                    right[h] = right[h] - ht * rows_r[t]
            out_l, out_r = rows_l[0], rows_r[0]
            for t in range(1, 8):
                out_l = jnp.where(sub == t, rows_l[t], out_l)
                out_r = jnp.where(sub == t, rows_r[t], out_r)
            a[base:base + 8, :NB] = out_l
            a[base:base + 8, NB:] = out_r
        hi = lo + SUB
        if hi < NB:
            got = a[lo:hi, :]
            sa, sb = stacks(got)
            a[hi:, :] = a[hi:, :] - tdot(sa[:, hi:NB], sb)


def chol_kernel(scale, g_ref, r_ref, w_ref, a):
    row = lax.broadcasted_iota(jnp.int32, (NB, NB), 0)
    col = lax.broadcasted_iota(jnp.int32, (NB, NB), 1)
    eye = (row == col).astype(F32)
    for i in range(KB):
        for j in range(i, KB):
            at = START[i, j]
            r_ref[NB * i:NB * (i + 1), NB * j:NB * (j + 1)] = g_ref[at:at + NB, :] * scale

    def step(k, _):
        here = pl.ds(pl.multiple_of(k * NB, NB), NB)
        a[:, :NB] = r_ref[here, here]
        a[:, NB:] = eye
        factor(a)
        w_ref[here, :] = a[:, NB:]
        r_ref[here, here] = jnp.where(col >= row, a[:, :NB], 0.0)
        for s in range(KB - 1):
            @pl.when(k == s)
            def _(s=s):
                lo = NB * (s + 1)
                panel = dot(a[:, NB:], r_ref[NB * s:lo, lo:], 1, 0)
                r_ref[NB * s:lo, lo:] = panel
                sa, sb = stacks(panel)
                for i in range(lo, N, 256):
                    n = min(256, N - i)
                    r_ref[i:i + n, i:] = r_ref[i:i + n, i:] - tdot(sa[:, i - lo:i - lo + n], sb[:, i - lo:])
        return 0

    lax.fori_loop(0, KB, step, 0)
    for i in range(1, KB):
        r_ref[NB * i:NB * (i + 1), :NB * i] = jnp.zeros((NB, NB * i), F32)


VM = pl.BlockSpec(memory_space=pltpu.VMEM)
HBM = pl.BlockSpec(memory_space=pltpu.HBM)
SM = pl.BlockSpec(memory_space=pltpu.SMEM)
PARAMS = pltpu.CompilerParams(vmem_limit_bytes=48 << 20)


def chol(packed, scale):
    return pl.pallas_call(
        functools.partial(chol_kernel, scale),
        out_shape=(jax.ShapeDtypeStruct((N, N), F32), jax.ShapeDtypeStruct((N, NB), F32)),
        in_specs=[VM],
        out_specs=(VM, VM),
        scratch_shapes=[pltpu.VMEM((NB, 2 * NB), F32)],
        compiler_params=PARAMS,
        cost_estimate=pl.CostEstimate(flops=1 << 33, bytes_accessed=8 << 20, transcendentals=0),
        name="chol",
    )(packed)


def thin_kernel(core_ref, y_ref, rm_ref, ro_ref, wm_ref, wo_ref, r_ref, out_ref, r, w, y, got, left, *, maker):
    def block(ref, k):
        return ref.at[pl.ds(k * NB, NB), :]

    def load(r_from, w_from):
        for k in range(KB):
            pltpu.make_async_copy(block(r_from, k), block(r, k), got.at[k]).start()
        w[...] = w_from[...]

    pl.when(core_ref[0] == maker)(lambda: load(rm_ref, wm_ref))
    pl.when(core_ref[0] != maker)(lambda: load(ro_ref, wo_ref))
    y[...] = y_ref[...]
    for k in range(KB):
        lo, hi = k * NB, (k + 1) * NB
        yk = dot(y[:, lo:hi], w[lo:hi, :], 1, 1)
        out_ref[:, lo:hi] = yk
        pltpu.make_async_copy(block(rm_ref, k), block(r, k), got.at[k]).wait()
        pltpu.make_async_copy(block(r, k), block(r_ref, k), left.at[k]).start()
        if hi < N:
            y[:, hi:] = y[:, hi:] - dot(yk, r[lo:hi, hi:], 1, 0)
    for k in range(KB):
        pltpu.make_async_copy(block(r, k), block(r_ref, k), left.at[k]).wait()


def thin(core, y, rm, ro, wm, wo, maker):
    return pl.pallas_call(
        functools.partial(thin_kernel, maker=maker),
        out_shape=(jax.ShapeDtypeStruct((N, N), F32), jax.ShapeDtypeStruct(y.shape, F32)),
        in_specs=[SM, VM, HBM, HBM, VM, VM],
        out_specs=(HBM, VM),
        scratch_shapes=[pltpu.VMEM((N, N), F32), pltpu.VMEM((N, NB), F32), pltpu.VMEM(y.shape, F32)] + [pltpu.SemaphoreType.DMA((KB,))] * 2,
        compiler_params=pltpu.CompilerParams(vmem_limit_bytes=60 << 20),
        name="thin",
    )(core, y, rm, ro, wm, wo)


def gram_kernel(core_ref, cu_ref, ci_ref, u_ref, i_ref, keep_ref, give_ref, counts, acc):
    eye = lax.broadcasted_iota(jnp.int32, (NB, NB), 0) == lax.broadcasted_iota(jnp.int32, (NB, NB), 1)

    def put(ref):
        for i, j in PAIRS_OF:
            at = START[i, j]
            ref[at:at + NB, :] = acc[NB * i:NB * (i + 1), NB * j:NB * (j + 1)]

    for maker, table in enumerate((u_ref, i_ref)):
        rows = table.shape[0]
        counts[:rows // NB, :] = ci_ref[...] if maker else cu_ref[...]
        for c in range(rows // CHUNK):
            blocks = range(c * (CHUNK // NB), (c + 1) * (CHUNK // NB))
            times = jnp.concatenate([jnp.sum(jnp.where(eye, counts[b:b + 1, :], 0.0), axis=1, keepdims=True) for b in blocks], 0)
            t = table[c * CHUNK:(c + 1) * CHUNK, :]
            weighted = t.astype(F32) * times
            high = weighted.astype(BF16)
            both = jnp.concatenate([high, (weighted - high.astype(F32)).astype(BF16)], 0)
            tt = jnp.concatenate([t, t], 0)
            for i in range(0, N, 256):
                got = tdot(tt[:, i:i + 256], both[:, i:])
                acc[i:i + 256, i:] = acc[i:i + 256, i:] + got if c else got
        pl.when(core_ref[0] == maker)(lambda: put(keep_ref))
        pl.when(core_ref[0] != maker)(lambda: put(give_ref))


def grams(core, user_counts, item_counts, user_table, item_table):
    packed = jax.ShapeDtypeStruct((36 * NB, NB), F32)
    return pl.pallas_call(
        gram_kernel,
        out_shape=(packed, packed),
        in_specs=[SM, VM, VM, VM, VM],
        out_specs=(VM, VM),
        scratch_shapes=[pltpu.VMEM((16, NB), F32), pltpu.VMEM((N, N), F32)],
        compiler_params=PARAMS,
        cost_estimate=pl.CostEstimate(flops=1 << 33, bytes_accessed=10 << 20, transcendentals=0),
        name="grams",
    )(core, user_counts, item_counts, user_table, item_table)


def spread_rows(src, dst, base):
    def tile(r, _):
        at = pl.multiple_of(r * 16, 16)
        for c in range(KB):
            dst[pl.ds((base + at) * KB + c, 16, stride=KB), :] = src[pl.ds(at, 16), NB * c:NB * (c + 1)].astype(F32)
        return 0

    lax.fori_loop(0, src.shape[0] // 16, tile, 0)


def gather_rows(src, dst):
    def tile(r, _):
        at = pl.multiple_of(r * 16, 16)
        for c in range(KB):
            dst[pl.ds(at, 16), NB * c:NB * (c + 1)] = src[pl.ds(at * KB + c, 16, stride=KB), :].astype(BF16)
        return 0

    lax.fori_loop(0, dst.shape[0] // 16, tile, 0)


def cross_kernel(core_ref, at_ref, col_ref, i_ref, *refs, groups, add, halves):
    tables, refs = refs[:sum(groups)], refs[sum(groups):]
    if add:
        old_ref, refs = refs[0], refs[1:]
    if halves:
        keep_ref, give_ref, uf, itf, pu, pi, panel, panel_i, out_ref = refs
    else:
        out_ref, uf, itf, pu, pi, panel, panel_i = refs
    spread_rows(i_ref, itf, 0)
    users = N
    uf[users * KB:, :] = jnp.zeros((KB, NB), F32)

    def group(g, _):
        first = 0
        for j, n in enumerate(groups):
            @pl.when(g == j)
            def _(first=first, n=n):
                base = 0
                for t in tables[first:first + n]:
                    spread_rows(t, uf, base)
                    base += t.shape[0]

            first += n

        def move(b, _):
            for k in range(8):
                s = b * 8 + k
                u = at_ref[g * SLOTS + s]
                i = col_ref[g * SLOTS + s]
                to = pl.ds(pl.multiple_of(s * KB, KB), KB)
                pu[to, :] = uf[pl.ds(pl.multiple_of(u * KB, KB), KB), :]
                pi[to, :] = itf[pl.ds(pl.multiple_of(i * KB, KB), KB), :]
            return 0

        lax.fori_loop(0, SLOTS // 8, move, 0)
        gather_rows(pu, panel)
        gather_rows(pi, panel_i)

        def block(b, _):
            rows = pl.ds(pl.multiple_of(b * 256, 256), 256)
            got = tdot(panel_i[:, rows], panel[...])
            if add and len(groups) == 1:
                out_ref[rows, :] = old_ref[rows, :] + got
            else:
                @pl.when(g == 0)
                def _():
                    out_ref[rows, :] = old_ref[rows, :] + got if add else got

                @pl.when(g > 0)
                def _():
                    out_ref[rows, :] = out_ref[rows, :] + got
            return 0

        lax.fori_loop(0, N // 256, block, 0)
        return 0

    lax.fori_loop(0, len(groups), group, 0)
    if halves:
        for c in range(2):
            @pl.when(core_ref[0] == c)
            def _(c=c):
                keep_ref[...] = out_ref[c * N // 2:(c + 1) * N // 2, :]
                give_ref[...] = out_ref[(1 - c) * N // 2:(2 - c) * N // 2, :]


def cross(core, at, cols, item_table, tables, groups, old=None, halves=False):
    items = item_table.shape[0]
    more = () if old is None else (old,)
    full, half = jax.ShapeDtypeStruct((N, N), F32), jax.ShapeDtypeStruct((N // 2, N), F32)
    return pl.pallas_call(
        functools.partial(cross_kernel, groups=groups, add=old is not None, halves=halves),
        out_shape=(half, half) if halves else full,
        in_specs=[SM, SM, SM] + [VM] * (1 + len(tables) + len(more)),
        out_specs=(VM, VM) if halves else VM,
        scratch_shapes=[
            pltpu.VMEM(((N + 1) * KB, NB), F32),
            pltpu.VMEM((items * KB, NB), F32),
            pltpu.VMEM((SLOTS * KB, NB), F32),
            pltpu.VMEM((SLOTS * KB, NB), F32),
            pltpu.VMEM((SLOTS, N), BF16),
            pltpu.VMEM((SLOTS, N), BF16),
        ] + ([pltpu.VMEM((N, N), F32)] if halves else []),
        compiler_params=pltpu.CompilerParams(vmem_limit_bytes=56 << 20),
        cost_estimate=pl.CostEstimate(flops=len(groups) << 32, bytes_accessed=12 << 20, transcendentals=0),
        name="cross",
    )(core, at, cols, item_table, *tables, *more)


CHIPS = ("y", "z", "x")
CORE_FIRST = ("core", "y", "z", "x")


def swap(b):
    return lax.ppermute(b, "core", [(0, 1), (1, 0)])


def histogram(key, bins):
    hot = (key[None, :] // NB == jnp.arange(bins // NB, dtype=jnp.int32)[:, None]) & (key >= 0)[None, :]
    lane = key[:, None] % NB == jnp.arange(NB, dtype=jnp.int32)[None, :]
    return lax.dot_general(hot.astype(BF16), lane.astype(BF16), (((1,), (0,)), ((), ())), preferred_element_type=F32)


def chip_scatter(b):
    return jnp.sum(lax.all_to_all(b, CHIPS, 0, 0, tiled=True), 0)


def chip_gather(b):
    return lax.all_to_all(jnp.broadcast_to(b[None], (64,) + b.shape), CHIPS, 0, 0, tiled=True)


def ring(k):
    return [(i, (i + k) % 4) for i in range(4)]


def shift(b, axis, k):
    return lax.ppermute(b, axis, ring(k % 4))


def slot_lists(pair_user, pair_item, pair_owner, pair_count, items):
    slots = pair_owner.shape[0]
    capacity = slots // 2
    keep = jnp.arange(slots, dtype=jnp.int32) < pair_count[0]
    owner = jnp.where(keep, pair_owner, -1)
    hot = (owner[None, :] == jnp.arange(4, dtype=jnp.int32)[:, None]).reshape(4, slots // NB, NB)
    tri = (jnp.arange(NB)[:, None] <= jnp.arange(NB)[None, :]).astype(BF16)
    inside = lax.dot_general(hot.astype(BF16), tri, (((2,), (0,)), ((), ())), preferred_element_type=F32)
    totals = inside[:, :, -1]
    before = jnp.cumsum(totals, axis=1) - totals
    rank = jnp.where(hot, inside + before[:, :, None] - 1.0, 0.0)
    place = jnp.sum(rank, axis=0).reshape(slots).astype(jnp.int32)
    flat = jnp.where(keep, owner * capacity + place, -1)
    code = pair_user * items + pair_item + 1
    spots = jnp.arange(4 * capacity, dtype=jnp.int32)
    return jnp.sum(jnp.where(flat[None, :] == spots[:, None], code[None, :], 0), axis=1).reshape(4, capacity)


def body(user_table, item_table, pair_user, pair_item, pair_owner, pair_count):
    users, width = user_table.shape
    items = item_table.shape[0]
    slots = pair_user.shape[0]
    total = float(slots * 128)
    core, x = lax.axis_index("core"), lax.axis_index("x")
    flag = core.reshape(1)

    codes = slot_lists(pair_user, pair_item, pair_owner, pair_count, items)
    named = codes > 0
    want = jnp.stack([jnp.where(named, (codes - 1) // items, -1), jnp.where(named, (codes - 1) % items, 0)], 1)
    got = lax.all_to_all(want, "x", 0, 0, tiled=True)
    lists = jnp.concatenate([lax.dynamic_slice_in_dim(got, (x + k) % 4, 1, 0) for k in (0, 3, 1, 2)], 0)
    rows, cols = lists[:, 0].reshape(-1), lists[:, 1].reshape(-1)

    user_table_sent, want = lax.optimization_barrier((user_table, want))
    left, right = shift(user_table_sent, "x", 1), shift(user_table_sent, "x", -1)
    far_a, far_b = shift(left[:users // 2], "x", 1), shift(right[users // 2:], "x", -1)

    keep = jnp.arange(slots, dtype=jnp.int32) < pair_count[0]
    user_counts = histogram(jnp.where(keep, pair_user, -1), users)
    item_counts = histogram(jnp.where(rows >= 0, cols, -1), items)
    keep_half, give_half = grams(flag, user_counts, item_counts, user_table, item_table)
    mine = keep_half + swap(give_half)
    mine = chip_scatter(mine.reshape(64, 72, NB))
    packed = chip_gather(mine).reshape(36 * NB, NB)

    spot = jnp.where(rows >= 0, rows, users)
    n = codes.shape[1]
    ct = cross(flag, spot[:n], cols[:n], item_table, (user_table,), (1,))
    ct = cross(flag, spot[n:3 * n], cols[n:3 * n], item_table, (left, right), (1, 1), ct)
    half, give = cross(flag, spot[3 * n:], cols[3 * n:], item_table, (far_a, far_b), (2,), ct, halves=True)
    half = half + swap(give)
    ct = chip_scatter(half.reshape(64, 8, width))

    r_mine, w_mine = chol(packed, 1.0 / total)
    r_other, w_other = swap(r_mine), swap(w_mine)
    r_user, left = thin(flag, ct * float(total) ** -0.5, r_mine, r_other, w_mine, w_other, 0)
    left = left.reshape(8, 4, 4, 2, 4, 8).transpose(3, 1, 2, 4, 0, 5).reshape(128, 64)
    left = lax.all_to_all(left, CORE_FIRST, 0, 0, tiled=True)
    left = left.reshape(width, 8).T
    r_item, whitened = thin(flag, left, r_mine, r_other, w_mine, w_other, 1)
    return (r_user, r_item, whitened)


def solution(mesh):
    fine = Mesh(mesh.devices.reshape(4, 4, 2, 4), ALL)
    placed = (P(ALL, None), P("x", None), P(ALL), P(ALL), P(ALL), P(ALL))

    return jax.shard_map(
        body,
        mesh=fine,
        in_specs=placed,
        out_specs=(P(), P(), P(ALL, None)),
        check_vma=False,
    )
```

```python
import functools

import jax
import jax.numpy as jnp
from jax import lax
from jax.experimental import pallas as pl
from jax.experimental.pallas import tpu as pltpu
from jax.sharding import Mesh, PartitionSpec as P


N = 1024
NB = 128
KB = N // NB
SUB = 32
CHUNK = 512
SLOTS = 1024
HI = lax.Precision.HIGHEST
F32 = jnp.float32
BF16 = jnp.bfloat16
PACKED = 36 * NB
ALL = ("y", "z", "core", "x")
PAIRS_OF = [(i, j) for i in range(KB) for j in range(i, KB)]
START = {ij: NB * n for n, ij in enumerate(PAIRS_OF)}


def row_of(v, t):
    return jnp.broadcast_to(v[t:t + 1, :], v.shape)


def lane_of(v, c):
    return jnp.broadcast_to(v[:, c:c + 1], (8, NB))


def dot(a, b, ca, cb):
    return lax.dot_general(a, b, (((ca,), (cb,)), ((), ())), precision=HI, preferred_element_type=F32)


def parts(a):
    h = a.astype(BF16)
    rest = a - h.astype(F32)
    m = rest.astype(BF16)
    return h, m, (rest - m.astype(F32)).astype(BF16)


def stacks(a):
    h, m, l = parts(a)
    return jnp.concatenate([h, h, m, m, h, l], 0), jnp.concatenate([h, m, h, m, l, h], 0)


def tdot(a, b):
    return lax.dot_general(a, b, (((0,), (0,)), ((), ())), preferred_element_type=F32)


def factor(a, tmp):
    sub = lax.broadcasted_iota(jnp.int32, (8, NB), 0)
    groups = SUB // 8
    for s in range(NB // SUB):
        lo = SUB * s
        left = [a[lo + 8 * g:lo + 8 * g + 8, :NB] for g in range(groups)]
        right = [a[lo + 8 * g:lo + 8 * g + 8, NB:] for g in range(groups)]
        for g in range(groups):
            base = lo + 8 * g
            cols = [lane_of(left[g], base + t) for t in range(8)]
            for t in range(8):
                tmp[8 * t:8 * t + 8, :] = cols[t]
            ent = {(u, t): tmp[pl.ds(8 * t + u, 8, stride=0), :] for t in range(8) for u in range(t, 8)}
            fac, inv = {}, []
            for t in range(8):
                ri = lax.rsqrt(ent[t, t])
                inv.append(ri)
                for u in range(t + 1, 8):
                    fac[t, u] = ent[u, t] * ri
                for v in range(t + 1, 8):
                    for u in range(v, 8):
                        ent[u, v] = ent[u, v] - fac[t, u] * fac[t, v]
            rows_l, rows_r = [], []
            for t in range(8):
                pl_, pr_ = row_of(left[g], t), row_of(right[g], t)
                for k in range(t):
                    pl_ = pl_ - fac[k, t] * rows_l[k]
                    pr_ = pr_ - fac[k, t] * rows_r[k]
                rows_l.append(pl_ * inv[t])
                rows_r.append(pr_ * inv[t])
            for h in range(g + 1, groups):
                hc = [lane_of(left[h], base + t) for t in range(8)]
                for t in range(8):
                    ht = hc[t] * inv[t]
                    for u in range(t + 1, 8):
                        hc[u] = hc[u] - ht * fac[t, u]
                    left[h] = left[h] - ht * rows_l[t]
                    right[h] = right[h] - ht * rows_r[t]
            out_l, out_r = rows_l[0], rows_r[0]
            for t in range(1, 8):
                out_l = jnp.where(sub == t, rows_l[t], out_l)
                out_r = jnp.where(sub == t, rows_r[t], out_r)
            a[base:base + 8, :NB] = out_l
            a[base:base + 8, NB:] = out_r
        hi = lo + SUB
        if hi < NB:
            got = a[lo:hi, :]
            sa, sb = stacks(got)
            a[hi:, :] = a[hi:, :] - tdot(sa[:, hi:NB], sb)


def chol_kernel(scale, g_ref, out_ref, gp, r, a, tmp, got):
    row = lax.broadcasted_iota(jnp.int32, (NB, NB), 0)
    col = lax.broadcasted_iota(jnp.int32, (NB, NB), 1)
    eye = (row == col).astype(F32)

    def fetch(i):
        rows = pl.ds(START[i, i], NB * (KB - i))
        return pltpu.make_async_copy(g_ref.at[rows, :], gp.at[rows, :], got.at[i])

    for i in range(KB):
        fetch(i).start()
    for i in range(KB):
        fetch(i).wait()
        for j in range(i, KB):
            r[NB * i:NB * (i + 1), NB * j:NB * (j + 1)] = gp[START[i, j]:START[i, j] + NB, :] * scale

    def step(k, _):
        at = pl.multiple_of(k * NB, NB)
        here = pl.ds(at, NB)
        a[:, :NB] = r[here, here]
        a[:, NB:] = eye
        factor(a, tmp)
        out_ref[pl.ds(PACKED + at, NB), :] = a[:, NB:]
        r[here, here] = jnp.where(col >= row, a[:, :NB], 0.0)
        for s in range(KB - 1):
            @pl.when(k == s)
            def _(s=s):
                lo = NB * (s + 1)
                panel = dot(a[:, NB:], r[NB * s:lo, lo:], 1, 0)
                r[NB * s:lo, lo:] = panel
                sa, sb = stacks(panel)
                for i in range(lo, N, 256):
                    n = min(256, N - i)
                    r[i:i + n, i:] = r[i:i + n, i:] - tdot(sa[:, i - lo:i - lo + n], sb[:, i - lo:])
        return 0

    lax.fori_loop(0, KB, step, 0)
    for i, j in PAIRS_OF:
        out_ref[START[i, j]:START[i, j] + NB, :] = r[NB * i:NB * (i + 1), NB * j:NB * (j + 1)]


VM = pl.BlockSpec(memory_space=pltpu.VMEM)
HBM = pl.BlockSpec(memory_space=pltpu.HBM)
SM = pl.BlockSpec(memory_space=pltpu.SMEM)
PARAMS = pltpu.CompilerParams(vmem_limit_bytes=28 << 20)


def chol(packed, scale):
    return pl.pallas_call(
        functools.partial(chol_kernel, scale),
        out_shape=jax.ShapeDtypeStruct((PACKED + N, NB), F32),
        in_specs=[HBM],
        out_specs=VM,
        scratch_shapes=[
            pltpu.VMEM((PACKED, NB), F32),
            pltpu.VMEM((N, N), F32),
            pltpu.VMEM((NB, 2 * NB), F32),
            pltpu.VMEM((8 * 8, NB), F32),
            pltpu.SemaphoreType.DMA((KB,)),
        ],
        compiler_params=PARAMS,
        cost_estimate=pl.CostEstimate(flops=1 << 33, bytes_accessed=8 << 20, transcendentals=0),
        name="chol",
    )(packed)


def place(m):
    core, chip, x = m // 64, m // 4 % 16, m % 4
    return (chip * 2 + core) * 4 + x


def thin_kernel(core_ref, y_ref, mine_ref, other_ref, r_ref, out_ref, rp, r, w, y, got, left, *, maker, scale):
    def rows(k):
        return pl.ds(START[k, k], NB * (KB - k))

    def fetch(src, k):
        return pltpu.make_async_copy(src.at[rows(k), :], rp.at[rows(k), :], got.at[k])

    def inverses(src):
        return pltpu.make_async_copy(src.at[pl.ds(PACKED, N), :], w, got.at[KB])

    def leave(k):
        block = pl.ds(k * NB, NB)
        return pltpu.make_async_copy(r.at[block, :], r_ref.at[block, :], left.at[k])

    def load(src):
        inverses(src).start()
        for k in range(KB):
            fetch(src, k).start()

    pl.when(core_ref[0] == maker)(lambda: load(mine_ref))
    pl.when(core_ref[0] != maker)(lambda: load(other_ref))
    if maker:
        for k in range(KB):
            y[:, NB * k:NB * (k + 1)] = jnp.transpose(y_ref[NB * k:NB * (k + 1), :])[:8, :]
    else:
        y[...] = y_ref[...] * scale
    inverses(mine_ref).wait()
    for k in range(KB):
        lo, hi = k * NB, (k + 1) * NB
        yk = dot(y[:, lo:hi], w[lo:hi, :], 1, 1)
        if maker:
            out_ref[:, lo:hi] = yk
        else:
            for m in range(128):
                at = place(m) * 8 - lo
                if 0 <= at < NB:
                    out_ref[m, :, :] = pltpu.roll(yk, (NB - at) % NB, 1) if at else yk
        fetch(mine_ref, k).wait()
        blocks = [rp[START[k, j]:START[k, j] + NB, :] for j in range(k, KB)]
        if hi < N:
            y[:, hi:] = y[:, hi:] - dot(yk, jnp.concatenate(blocks[1:], 1), 1, 0)
            r[hi:, lo:hi] = jnp.zeros((N - hi, NB), F32)
        for j in range(k, KB):
            r[lo:hi, NB * j:NB * (j + 1)] = blocks[j - k]
        leave(k).start()
    for k in range(KB):
        leave(k).wait()


def thin(core, y, mine, other, maker, scale=1.0):
    out = (8, N) if maker else (128, 8, NB)
    return pl.pallas_call(
        functools.partial(thin_kernel, maker=maker, scale=scale),
        out_shape=(jax.ShapeDtypeStruct((N, N), F32), jax.ShapeDtypeStruct(out, F32)),
        in_specs=[SM, VM, HBM, HBM],
        out_specs=(HBM, VM),
        scratch_shapes=[
            pltpu.VMEM((PACKED, NB), F32),
            pltpu.VMEM((N, N), F32),
            pltpu.VMEM((N, NB), F32),
            pltpu.VMEM((8, N), F32),
            pltpu.SemaphoreType.DMA((KB + 1,)),
            pltpu.SemaphoreType.DMA((KB,)),
        ],
        compiler_params=pltpu.CompilerParams(vmem_limit_bytes=60 << 20),
        name="thin",
    )(core, y, mine, other)


def gram_kernel(core_ref, cu_ref, ci_ref, u_ref, i_ref, keep_ref, give_ref, counts, acc):
    eye = lax.broadcasted_iota(jnp.int32, (NB, NB), 0) == lax.broadcasted_iota(jnp.int32, (NB, NB), 1)

    def put(ref):
        for i, j in PAIRS_OF:
            at = START[i, j]
            ref[at:at + NB, :] = acc[NB * i:NB * (i + 1), NB * j:NB * (j + 1)]

    for maker, table in enumerate((u_ref, i_ref)):
        rows = table.shape[0]
        counts[:rows // NB, :] = ci_ref[...] if maker else cu_ref[...]
        acc[...] = jnp.zeros((N, N), F32)

        def chunk(c):
            times = [jnp.sum(jnp.where(eye, counts[pl.ds(c * (CHUNK // NB) + b, 1), :], 0.0), axis=1, keepdims=True) for b in range(CHUNK // NB)]
            t = table[pl.ds(pl.multiple_of(c * CHUNK, CHUNK), CHUNK), :]
            weighted = t.astype(F32) * jnp.concatenate(times, 0)
            high = weighted.astype(BF16)
            both = jnp.concatenate([high, (weighted - high.astype(F32)).astype(BF16)], 0)
            tt = jnp.concatenate([t, t], 0)
            for i in range(0, N, 256):
                acc[i:i + 256, i:] = acc[i:i + 256, i:] + tdot(tt[:, i:i + 256], both[:, i:])

        def chunks(c, _):
            for k in range(1 + maker):
                chunk(c * (1 + maker) + k)
            return 0

        lax.fori_loop(0, 2, chunks, 0)
        pl.when(core_ref[0] == maker)(lambda: put(keep_ref))
        pl.when(core_ref[0] != maker)(lambda: put(give_ref))


def grams(core, user_counts, item_counts, user_table, item_table):
    packed = jax.ShapeDtypeStruct((36 * NB, NB), F32)
    return pl.pallas_call(
        gram_kernel,
        out_shape=(packed, packed),
        in_specs=[SM, VM, VM, VM, VM],
        out_specs=(VM, VM),
        scratch_shapes=[pltpu.VMEM((16, NB), F32), pltpu.VMEM((N, N), F32)],
        compiler_params=PARAMS,
        cost_estimate=pl.CostEstimate(flops=1 << 33, bytes_accessed=10 << 20, transcendentals=0),
        name="grams",
    )(core, user_counts, item_counts, user_table, item_table)


def spread_rows(src, dst, base):
    def tile(r, _):
        at = pl.multiple_of(r * 16, 16)
        for c in range(KB):
            dst[pl.ds((base + at) * KB + c, 16, stride=KB), :] = src[pl.ds(at, 16), NB * c:NB * (c + 1)].astype(F32)
        return 0

    lax.fori_loop(0, src.shape[0] // 16, tile, 0)


def gather_rows(src, dst):
    def tile(r, _):
        at = pl.multiple_of(r * 16, 16)
        for c in range(KB):
            dst[pl.ds(at, 16), NB * c:NB * (c + 1)] = src[pl.ds(at * KB + c, 16, stride=KB), :].astype(BF16)
        return 0

    lax.fori_loop(0, dst.shape[0] // 16, tile, 0)


def cross_kernel(core_ref, at_ref, col_ref, i_ref, *refs, groups, add, halves):
    tables, refs = refs[:sum(groups)], refs[sum(groups):]
    if add:
        old_ref, refs = refs[0], refs[1:]
    if halves:
        keep_ref, give_ref, uf, itf, pu, pi, panel, panel_i, out_ref = refs
    else:
        out_ref, uf, itf, pu, pi, panel, panel_i = refs
    spread_rows(i_ref, itf, 0)
    users = N
    uf[users * KB:, :] = jnp.zeros((KB, NB), F32)

    def group(g, _):
        first = 0
        for j, n in enumerate(groups):
            @pl.when(g == j)
            def _(first=first, n=n):
                base = 0
                for t in tables[first:first + n]:
                    spread_rows(t, uf, base)
                    base += t.shape[0]

            first += n

        def move(b, _):
            for k in range(8):
                s = b * 8 + k
                u = at_ref[g * SLOTS + s]
                i = col_ref[g * SLOTS + s]
                to = pl.ds(pl.multiple_of(s * KB, KB), KB)
                pu[to, :] = uf[pl.ds(pl.multiple_of(u * KB, KB), KB), :]
                pi[to, :] = itf[pl.ds(pl.multiple_of(i * KB, KB), KB), :]
            return 0

        lax.fori_loop(0, SLOTS // 8, move, 0)
        gather_rows(pu, panel)
        gather_rows(pi, panel_i)

        def block(b, _):
            rows = pl.ds(pl.multiple_of(b * 256, 256), 256)
            got = tdot(panel_i[:, rows], panel[...])
            if add and len(groups) == 1:
                out_ref[rows, :] = old_ref[rows, :] + got
            else:
                @pl.when(g == 0)
                def _():
                    out_ref[rows, :] = old_ref[rows, :] + got if add else got

                @pl.when(g > 0)
                def _():
                    out_ref[rows, :] = out_ref[rows, :] + got
            return 0

        lax.fori_loop(0, N // 256, block, 0)
        return 0

    lax.fori_loop(0, len(groups), group, 0)
    if halves:
        for c in range(2):
            @pl.when(core_ref[0] == c)
            def _(c=c):
                keep_ref[...] = out_ref[c * N // 2:(c + 1) * N // 2, :]
                give_ref[...] = out_ref[(1 - c) * N // 2:(2 - c) * N // 2, :]


def cross(core, at, cols, item_table, tables, groups, old=None, halves=False):
    items = item_table.shape[0]
    more = () if old is None else (old,)
    full, half = jax.ShapeDtypeStruct((N, N), F32), jax.ShapeDtypeStruct((N // 2, N), F32)
    return pl.pallas_call(
        functools.partial(cross_kernel, groups=groups, add=old is not None, halves=halves),
        out_shape=(half, half) if halves else full,
        in_specs=[SM, SM, SM] + [VM] * (1 + len(tables) + len(more)),
        out_specs=(VM, VM) if halves else VM,
        scratch_shapes=[
            pltpu.VMEM(((N + 1) * KB, NB), F32),
            pltpu.VMEM((items * KB, NB), F32),
            pltpu.VMEM((SLOTS * KB, NB), F32),
            pltpu.VMEM((SLOTS * KB, NB), F32),
            pltpu.VMEM((SLOTS, N), BF16),
            pltpu.VMEM((SLOTS, N), BF16),
        ] + ([pltpu.VMEM((N, N), F32)] if halves else []),
        compiler_params=pltpu.CompilerParams(vmem_limit_bytes=56 << 20),
        cost_estimate=pl.CostEstimate(flops=len(groups) << 32, bytes_accessed=12 << 20, transcendentals=0),
        name="cross",
    )(core, at, cols, item_table, *tables, *more)


CHIPS = ("y", "z", "x")
CORE_FIRST = ("core", "y", "z", "x")


def swap(b):
    return lax.ppermute(b, "core", [(0, 1), (1, 0)])


def histogram(key, bins):
    hot = (key[None, :] // NB == jnp.arange(bins // NB, dtype=jnp.int32)[:, None]) & (key >= 0)[None, :]
    lane = key[:, None] % NB == jnp.arange(NB, dtype=jnp.int32)[None, :]
    return lax.dot_general(hot.astype(BF16), lane.astype(BF16), (((1,), (0,)), ((), ())), preferred_element_type=F32)


def chip_scatter(b):
    return jnp.sum(lax.all_to_all(b, CHIPS, 0, 0, tiled=True), 0)


def chip_gather(b):
    return lax.all_to_all(jnp.broadcast_to(b[None], (64,) + b.shape), CHIPS, 0, 0, tiled=True)


def ring(k):
    return [(i, (i + k) % 4) for i in range(4)]


def shift(b, axis, k):
    return lax.ppermute(b, axis, ring(k % 4))


def slot_lists(pair_user, pair_item, pair_owner, pair_count, items):
    slots = pair_owner.shape[0]
    capacity = slots // 2
    keep = jnp.arange(slots, dtype=jnp.int32) < pair_count[0]
    owner = jnp.where(keep, pair_owner, -1)
    hot = (owner[None, :] == jnp.arange(4, dtype=jnp.int32)[:, None]).reshape(4, slots // NB, NB)
    tri = (jnp.arange(NB)[:, None] <= jnp.arange(NB)[None, :]).astype(BF16)
    inside = lax.dot_general(hot.astype(BF16), tri, (((2,), (0,)), ((), ())), preferred_element_type=F32)
    totals = inside[:, :, -1]
    before = jnp.cumsum(totals, axis=1) - totals
    rank = jnp.where(hot, inside + before[:, :, None] - 1.0, 0.0)
    place = jnp.sum(rank, axis=0).reshape(slots).astype(jnp.int32)
    flat = jnp.where(keep, owner * capacity + place, -1)
    code = pair_user * items + pair_item + 1
    spots = jnp.arange(4 * capacity, dtype=jnp.int32)
    return jnp.sum(jnp.where(flat[None, :] == spots[:, None], code[None, :], 0), axis=1).reshape(4, capacity)


def body(user_table, item_table, pair_user, pair_item, pair_owner, pair_count):
    users, width = user_table.shape
    items = item_table.shape[0]
    slots = pair_user.shape[0]
    total = float(slots * 128)
    core, x = lax.axis_index("core"), lax.axis_index("x")
    flag = core.reshape(1)

    codes = slot_lists(pair_user, pair_item, pair_owner, pair_count, items)
    named = codes > 0
    want = jnp.stack([jnp.where(named, (codes - 1) // items, -1), jnp.where(named, (codes - 1) % items, 0)], 1)
    got = lax.all_to_all(want, "x", 0, 0, tiled=True)
    lists = jnp.concatenate([lax.dynamic_slice_in_dim(got, (x + k) % 4, 1, 0) for k in (0, 3, 1, 2)], 0)
    rows, cols = lists[:, 0].reshape(-1), lists[:, 1].reshape(-1)

    user_table_sent, want = lax.optimization_barrier((user_table, want))
    left, right = shift(user_table_sent, "x", 1), shift(user_table_sent, "x", -1)
    far_a, far_b = shift(left[:users // 2], "x", 1), shift(right[users // 2:], "x", -1)

    keep = jnp.arange(slots, dtype=jnp.int32) < pair_count[0]
    user_counts = histogram(jnp.where(keep, pair_user, -1), users)
    item_counts = histogram(jnp.where(rows >= 0, cols, -1), items)
    keep_half, give_half = grams(flag, user_counts, item_counts, user_table, item_table)
    mine = keep_half + swap(give_half)
    mine = chip_scatter(mine.reshape(64, 72, NB))
    packed = chip_gather(mine).reshape(36 * NB, NB)

    spot = jnp.where(rows >= 0, rows, users)
    n = codes.shape[1]
    ct = cross(flag, spot[:n], cols[:n], item_table, (user_table,), (1,))
    ct = cross(flag, spot[n:3 * n], cols[n:3 * n], item_table, (left, right), (1, 1), ct)
    half, give = cross(flag, spot[3 * n:], cols[3 * n:], item_table, (far_a, far_b), (2,), ct, halves=True)
    half = half + swap(give)
    ct = chip_scatter(half.reshape(64, 8, width))

    mine = chol(packed, 1.0 / total)
    other = swap(mine)
    r_user, left = thin(flag, ct, mine, other, 0, float(total) ** -0.5)
    left = lax.all_to_all(left, CORE_FIRST, 0, 0, tiled=True).reshape(width, NB)
    r_item, whitened = thin(flag, left, mine, other, 1)
    return (r_user, r_item, whitened)


def solution(mesh):
    fine = Mesh(mesh.devices.reshape(4, 4, 2, 4), ALL)
    placed = (P(ALL, None), P("x", None), P(ALL), P(ALL), P(ALL), P(ALL))

    return jax.shard_map(
        body,
        mesh=fine,
        in_specs=placed,
        out_specs=(P(), P(), P(ALL, None)),
        check_vma=False,
    )
```

```python
import functools

import jax
import jax.numpy as jnp
from jax import lax
from jax.experimental import pallas as pl
from jax.experimental.pallas import tpu as pltpu
from jax.sharding import Mesh, PartitionSpec as P


N = 1024
NB = 128
KB = N // NB
SUB = 32
CHUNK = 512
SLOTS = 1024
HI = lax.Precision.HIGHEST
F32 = jnp.float32
BF16 = jnp.bfloat16
PACKED = 36 * NB
ALL = ("y", "z", "core", "x")
PAIRS_OF = [(i, j) for i in range(KB) for j in range(i, KB)]
START = {ij: NB * n for n, ij in enumerate(PAIRS_OF)}


def row_of(v, t):
    return jnp.broadcast_to(v[t:t + 1, :], v.shape)


def lane_of(v, c):
    return jnp.broadcast_to(v[:, c:c + 1], (8, NB))


def dot(a, b, ca, cb):
    return lax.dot_general(a, b, (((ca,), (cb,)), ((), ())), precision=HI, preferred_element_type=F32)


def parts(a):
    h = a.astype(BF16)
    rest = a - h.astype(F32)
    m = rest.astype(BF16)
    return h, m, (rest - m.astype(F32)).astype(BF16)


def stacks(a):
    h, m, l = parts(a)
    return jnp.concatenate([h, h, m, m, h, l], 0), jnp.concatenate([h, m, h, m, l, h], 0)


def tdot(a, b):
    return lax.dot_general(a, b, (((0,), (0,)), ((), ())), preferred_element_type=F32)


def factor(a, tmp):
    sub = lax.broadcasted_iota(jnp.int32, (8, NB), 0)
    groups = SUB // 8
    for s in range(NB // SUB):
        lo = SUB * s
        left = [a[lo + 8 * g:lo + 8 * g + 8, :NB] for g in range(groups)]
        right = [a[lo + 8 * g:lo + 8 * g + 8, NB:] for g in range(groups)]
        for g in range(groups):
            base = lo + 8 * g
            cols = [lane_of(left[g], base + t) for t in range(8)]
            for t in range(8):
                tmp[8 * t:8 * t + 8, :] = cols[t]
            ent = {(u, t): tmp[pl.ds(8 * t + u, 8, stride=0), :] for t in range(8) for u in range(t, 8)}
            fac, inv = {}, []
            for t in range(8):
                ri = lax.rsqrt(ent[t, t])
                inv.append(ri)
                for u in range(t + 1, 8):
                    fac[t, u] = ent[u, t] * ri
                for v in range(t + 1, 8):
                    for u in range(v, 8):
                        ent[u, v] = ent[u, v] - fac[t, u] * fac[t, v]
            rows_l, rows_r = [], []
            for t in range(8):
                pl_, pr_ = row_of(left[g], t), row_of(right[g], t)
                for k in range(t):
                    pl_ = pl_ - fac[k, t] * rows_l[k]
                    pr_ = pr_ - fac[k, t] * rows_r[k]
                rows_l.append(pl_ * inv[t])
                rows_r.append(pr_ * inv[t])
            for h in range(g + 1, groups):
                hc = [lane_of(left[h], base + t) for t in range(8)]
                for t in range(8):
                    ht = hc[t] * inv[t]
                    for u in range(t + 1, 8):
                        hc[u] = hc[u] - ht * fac[t, u]
                    left[h] = left[h] - ht * rows_l[t]
                    right[h] = right[h] - ht * rows_r[t]
            out_l, out_r = rows_l[0], rows_r[0]
            for t in range(1, 8):
                out_l = jnp.where(sub == t, rows_l[t], out_l)
                out_r = jnp.where(sub == t, rows_r[t], out_r)
            a[base:base + 8, :NB] = out_l
            a[base:base + 8, NB:] = out_r
        hi = lo + SUB
        if hi < NB:
            got = a[lo:hi, :]
            sa, sb = stacks(got)
            a[hi:, :] = a[hi:, :] - tdot(sa[:, hi:NB], sb)


def chol_kernel(scale, g_ref, out_ref, gp, r, a, tmp, got):
    row = lax.broadcasted_iota(jnp.int32, (NB, NB), 0)
    col = lax.broadcasted_iota(jnp.int32, (NB, NB), 1)
    eye = (row == col).astype(F32)

    def fetch(i):
        rows = pl.ds(START[i, i], NB * (KB - i))
        return pltpu.make_async_copy(g_ref.at[rows, :], gp.at[rows, :], got.at[i])

    for i in range(KB):
        fetch(i).start()
    for i in range(KB):
        fetch(i).wait()
        for j in range(i, KB):
            r[NB * i:NB * (i + 1), NB * j:NB * (j + 1)] = gp[START[i, j]:START[i, j] + NB, :] * scale

    def step(k, _):
        at = pl.multiple_of(k * NB, NB)
        here = pl.ds(at, NB)
        a[:, :NB] = r[here, here]
        a[:, NB:] = eye
        factor(a, tmp)
        out_ref[pl.ds(PACKED + at, NB), :] = a[:, NB:]
        r[here, here] = jnp.where(col >= row, a[:, :NB], 0.0)
        for s in range(KB - 1):
            @pl.when(k == s)
            def _(s=s):
                lo = NB * (s + 1)
                panel = dot(a[:, NB:], r[NB * s:lo, lo:], 1, 0)
                r[NB * s:lo, lo:] = panel
                sa, sb = stacks(panel)
                for i in range(lo, N, 256):
                    n = min(256, N - i)
                    r[i:i + n, i:] = r[i:i + n, i:] - tdot(sa[:, i - lo:i - lo + n], sb[:, i - lo:])
        return 0

    lax.fori_loop(0, KB, step, 0)
    for i, j in PAIRS_OF:
        out_ref[START[i, j]:START[i, j] + NB, :] = r[NB * i:NB * (i + 1), NB * j:NB * (j + 1)]


VM = pl.BlockSpec(memory_space=pltpu.VMEM)
HBM = pl.BlockSpec(memory_space=pltpu.HBM)
SM = pl.BlockSpec(memory_space=pltpu.SMEM)
PARAMS = pltpu.CompilerParams(vmem_limit_bytes=28 << 20)


def chol(packed, scale):
    return pl.pallas_call(
        functools.partial(chol_kernel, scale),
        out_shape=jax.ShapeDtypeStruct((PACKED + N, NB), F32),
        in_specs=[HBM],
        out_specs=VM,
        scratch_shapes=[
            pltpu.VMEM((PACKED, NB), F32),
            pltpu.VMEM((N, N), F32),
            pltpu.VMEM((NB, 2 * NB), F32),
            pltpu.VMEM((8 * 8, NB), F32),
            pltpu.SemaphoreType.DMA((KB,)),
        ],
        compiler_params=pltpu.CompilerParams(vmem_limit_bytes=60 << 20),
        cost_estimate=pl.CostEstimate(flops=1 << 33, bytes_accessed=8 << 20, transcendentals=0),
        name="chol",
    )(packed)


def small_dot(y, b, cb):
    low = y - y.astype(BF16).astype(F32)
    tail = low - low.astype(BF16).astype(F32)
    rows = jnp.concatenate([y, low, tail, jnp.zeros_like(y)], 0).astype(BF16)
    p, q, t = [lax.dot_general(rows, part, (((1,), (cb,)), ((), ())), preferred_element_type=F32) for part in parts(b)]
    return p[:8] + ((p[8:16] + q[:8]) + (p[16:24] + q[8:16] + t[:8]))


def place(m):
    core, chip, x = m // 64, m // 4 % 16, m % 4
    return (chip * 2 + core) * 4 + x


def thin_kernel(core_ref, y_ref, mine_ref, other_ref, r_ref, out_ref, rp, r, w, y, got, left, *, maker, scale):
    def rows(k):
        return pl.ds(START[k, k], NB * (KB - k))

    def fetch(src, k):
        return pltpu.make_async_copy(src.at[rows(k), :], rp.at[rows(k), :], got.at[k])

    def inverses(src):
        return pltpu.make_async_copy(src.at[pl.ds(PACKED, N), :], w, got.at[KB])

    def leave(k):
        block = pl.ds(k * NB, NB)
        return pltpu.make_async_copy(r.at[block, :], r_ref.at[block, :], left.at[k])

    def load(src):
        inverses(src).start()
        for k in range(KB):
            fetch(src, k).start()

    pl.when(core_ref[0] == maker)(lambda: load(mine_ref))
    pl.when(core_ref[0] != maker)(lambda: load(other_ref))
    if maker:
        for k in range(KB):
            y[:, NB * k:NB * (k + 1)] = jnp.transpose(y_ref[NB * k:NB * (k + 1), :])[:8, :]
    else:
        y[...] = y_ref[...] * scale
    inverses(mine_ref).wait()
    for k in range(KB):
        lo, hi = k * NB, (k + 1) * NB
        yk = small_dot(y[:, lo:hi], w[lo:hi, :], 1)
        if maker:
            out_ref[:, lo:hi] = yk
        else:
            for m in range(128):
                at = place(m) * 8 - lo
                if 0 <= at < NB:
                    out_ref[m, :, :] = pltpu.roll(yk, (NB - at) % NB, 1) if at else yk
        fetch(mine_ref, k).wait()
        blocks = [rp[START[k, j]:START[k, j] + NB, :] for j in range(k, KB)]
        if hi < N:
            y[:, hi:] = y[:, hi:] - small_dot(yk, jnp.concatenate(blocks[1:], 1), 0)
            r[hi:, lo:hi] = jnp.zeros((N - hi, NB), F32)
        for j in range(k, KB):
            r[lo:hi, NB * j:NB * (j + 1)] = blocks[j - k]
        leave(k).start()
    for k in range(KB):
        leave(k).wait()


def thin(core, y, mine, other, maker, scale=1.0):
    out = (8, N) if maker else (128, 8, NB)
    return pl.pallas_call(
        functools.partial(thin_kernel, maker=maker, scale=scale),
        out_shape=(jax.ShapeDtypeStruct((N, N), F32), jax.ShapeDtypeStruct(out, F32)),
        in_specs=[SM, VM, HBM, HBM],
        out_specs=(HBM, VM),
        scratch_shapes=[
            pltpu.VMEM((PACKED, NB), F32),
            pltpu.VMEM((N, N), F32),
            pltpu.VMEM((N, NB), F32),
            pltpu.VMEM((8, N), F32),
            pltpu.SemaphoreType.DMA((KB + 1,)),
            pltpu.SemaphoreType.DMA((KB,)),
        ],
        compiler_params=pltpu.CompilerParams(vmem_limit_bytes=60 << 20),
        name="thin",
    )(core, y, mine, other)


def gram_kernel(core_ref, cu_ref, ci_ref, u_ref, i_ref, keep_ref, give_ref, counts, acc):
    eye = lax.broadcasted_iota(jnp.int32, (NB, NB), 0) == lax.broadcasted_iota(jnp.int32, (NB, NB), 1)

    def put(ref):
        for i, j in PAIRS_OF:
            at = START[i, j]
            ref[at:at + NB, :] = acc[NB * i:NB * (i + 1), NB * j:NB * (j + 1)]

    for maker, table in enumerate((u_ref, i_ref)):
        rows = table.shape[0]
        counts[:rows // NB, :] = ci_ref[...] if maker else cu_ref[...]
        acc[...] = jnp.zeros((N, N), F32)

        def chunk(c):
            times = [jnp.sum(jnp.where(eye, counts[pl.ds(c * (CHUNK // NB) + b, 1), :], 0.0), axis=1, keepdims=True) for b in range(CHUNK // NB)]
            t = table[pl.ds(pl.multiple_of(c * CHUNK, CHUNK), CHUNK), :]
            weighted = t.astype(F32) * jnp.concatenate(times, 0)
            high = weighted.astype(BF16)
            both = jnp.concatenate([high, (weighted - high.astype(F32)).astype(BF16)], 0)
            tt = jnp.concatenate([t, t], 0)
            for i in range(0, N, 256):
                acc[i:i + 256, i:] = acc[i:i + 256, i:] + tdot(tt[:, i:i + 256], both[:, i:])

        def chunks(c, _):
            for k in range(1 + maker):
                chunk(c * (1 + maker) + k)
            return 0

        lax.fori_loop(0, 2, chunks, 0)
        pl.when(core_ref[0] == maker)(lambda: put(keep_ref))
        pl.when(core_ref[0] != maker)(lambda: put(give_ref))


def grams(core, user_counts, item_counts, user_table, item_table):
    packed = jax.ShapeDtypeStruct((36 * NB, NB), F32)
    return pl.pallas_call(
        gram_kernel,
        out_shape=(packed, packed),
        in_specs=[SM, VM, VM, VM, VM],
        out_specs=(VM, VM),
        scratch_shapes=[pltpu.VMEM((16, NB), F32), pltpu.VMEM((N, N), F32)],
        compiler_params=PARAMS,
        cost_estimate=pl.CostEstimate(flops=1 << 33, bytes_accessed=10 << 20, transcendentals=0),
        name="grams",
    )(core, user_counts, item_counts, user_table, item_table)


def spread_rows(src, dst):
    def tile(r, _):
        at = pl.multiple_of(r * 16, 16)
        for c in range(KB):
            dst[pl.ds(at * KB + c, 16, stride=KB), :] = src[pl.ds(at, 16), NB * c:NB * (c + 1)].astype(F32)
        return 0

    lax.fori_loop(0, src.shape[0] // 16, tile, 0)


def gather_rows(src, dst):
    def tile(r, _):
        at = pl.multiple_of(r * 16, 16)
        for c in range(KB):
            dst[pl.ds(at, 16), NB * c:NB * (c + 1)] = src[pl.ds(at * KB + c, 16, stride=KB), :].astype(BF16)
        return 0

    lax.fori_loop(0, dst.shape[0] // 16, tile, 0)


def cross_kernel(core_ref, at_ref, col_ref, i_ref, *refs, groups, add, halves):
    count = sum(groups)
    tables, refs = refs[:count], refs[count:]
    if add:
        old_ref, refs = refs[0], refs[1:]
    outs, refs = refs[:1 + halves], refs[1 + halves:]
    ib, ub, uf, itf, pu, pi, panel, panel_i, acc, got_i, got_u, got_old, left = refs
    last = len(groups) - 1
    spots = [(g, t) for g, n in enumerate(groups) for t in range(n)]

    def item_copy():
        return pltpu.make_async_copy(i_ref, ib, got_i)

    def old_copy():
        return pltpu.make_async_copy(old_ref, acc, got_old)

    def table_copy(n):
        g, t = spots[n]
        rows = tables[n].shape[0]
        return pltpu.make_async_copy(tables[n], ub.at[g, pl.ds(t * rows, rows), :], got_u.at[n])

    def leave(b, ref, to):
        rows = pl.ds(pl.multiple_of(b * 256, 256), 256)
        return pltpu.make_async_copy(acc.at[rows, :], ref.at[pl.ds(pl.multiple_of(to * 256, 256), 256), :], left.at[b])

    item_copy().start()
    for n in range(count):
        table_copy(n).start()
    if add:
        old_copy().start()
    item_copy().wait()
    spread_rows(ib, itf)
    uf[N * KB:, :] = jnp.zeros((KB, NB), F32)

    def group(g, _):
        for j in range(len(groups)):
            @pl.when(g == j)
            def _(j=j):
                for n in range(count):
                    if spots[n][0] == j:
                        table_copy(n).wait()
                spread_rows(ub.at[j], uf)

        def move(b, _):
            for k in range(8):
                s = b * 8 + k
                u = at_ref[g * SLOTS + s]
                i = col_ref[g * SLOTS + s]
                to = pl.ds(pl.multiple_of(s * KB, KB), KB)
                pu[to, :] = uf[pl.ds(pl.multiple_of(u * KB, KB), KB), :]
                pi[to, :] = itf[pl.ds(pl.multiple_of(i * KB, KB), KB), :]
            return 0

        lax.fori_loop(0, SLOTS // 8, move, 0)
        gather_rows(pu, panel)
        gather_rows(pi, panel_i)
        if add:
            @pl.when(g == 0)
            def _():
                old_copy().wait()

        def block(b, _):
            rows = pl.ds(pl.multiple_of(b * 256, 256), 256)
            got = tdot(panel_i[:, rows], panel[...])
            if add:
                acc[rows, :] = acc[rows, :] + got
            else:
                acc[rows, :] = got

            @pl.when(g == last)
            def _():
                if halves:
                    mine = b // 2 == core_ref[0]
                    pl.when(mine)(lambda: leave(b, outs[0], b % 2).start())
                    pl.when(jnp.logical_not(mine))(lambda: leave(b, outs[1], b % 2).start())
                else:
                    leave(b, outs[0], b).start()

            return 0

        lax.fori_loop(0, N // 256, block, 0)
        return 0

    lax.fori_loop(0, len(groups), group, 0)
    for b in range(N // 256):
        leave(b, outs[0], 0).wait()


def cross(core, at, cols, item_table, tables, groups, old=None, halves=False):
    assert old is not None or len(groups) == 1
    items = item_table.shape[0]
    more = () if old is None else (old,)
    full, half = jax.ShapeDtypeStruct((N, N), F32), jax.ShapeDtypeStruct((N // 2, N), F32)
    return pl.pallas_call(
        functools.partial(cross_kernel, groups=groups, add=old is not None, halves=halves),
        out_shape=(half, half) if halves else full,
        in_specs=[SM, SM, SM] + [HBM] * (1 + len(tables) + len(more)),
        out_specs=(HBM, HBM) if halves else HBM,
        scratch_shapes=[
            pltpu.VMEM((items, N), BF16),
            pltpu.VMEM((len(groups), N, N), BF16),
            pltpu.VMEM(((N + 1) * KB, NB), F32),
            pltpu.VMEM((items * KB, NB), F32),
            pltpu.VMEM((SLOTS * KB, NB), F32),
            pltpu.VMEM((SLOTS * KB, NB), F32),
            pltpu.VMEM((SLOTS, N), BF16),
            pltpu.VMEM((SLOTS, N), BF16),
            pltpu.VMEM((N, N), F32),
            pltpu.SemaphoreType.DMA,
            pltpu.SemaphoreType.DMA((len(tables),)),
            pltpu.SemaphoreType.DMA,
            pltpu.SemaphoreType.DMA((N // 256,)),
        ],
        compiler_params=pltpu.CompilerParams(vmem_limit_bytes=60 << 20),
        cost_estimate=pl.CostEstimate(flops=len(groups) << 32, bytes_accessed=12 << 20, transcendentals=0),
        name="cross",
    )(core, at, cols, item_table, *tables, *more)


CHIPS = ("y", "z", "x")
CORE_FIRST = ("core", "y", "z", "x")


def swap(b):
    return lax.ppermute(b, "core", [(0, 1), (1, 0)])


def histogram(key, bins):
    hot = (key[None, :] // NB == jnp.arange(bins // NB, dtype=jnp.int32)[:, None]) & (key >= 0)[None, :]
    lane = key[:, None] % NB == jnp.arange(NB, dtype=jnp.int32)[None, :]
    return lax.dot_general(hot.astype(BF16), lane.astype(BF16), (((1,), (0,)), ((), ())), preferred_element_type=F32)


def chip_scatter(b):
    return jnp.sum(lax.all_to_all(b, CHIPS, 0, 0, tiled=True), 0)


def chip_gather(b):
    return lax.all_to_all(jnp.broadcast_to(b[None], (64,) + b.shape), CHIPS, 0, 0, tiled=True)


def ring(k):
    return [(i, (i + k) % 4) for i in range(4)]


def shift(b, axis, k):
    return lax.ppermute(b, axis, ring(k % 4))


def slot_lists(pair_user, pair_item, pair_owner, pair_count, items):
    slots = pair_owner.shape[0]
    capacity = slots // 2
    keep = jnp.arange(slots, dtype=jnp.int32) < pair_count[0]
    owner = jnp.where(keep, pair_owner, -1)
    hot = (owner[None, :] == jnp.arange(4, dtype=jnp.int32)[:, None]).reshape(4, slots // NB, NB)
    tri = (jnp.arange(NB)[:, None] <= jnp.arange(NB)[None, :]).astype(BF16)
    inside = lax.dot_general(hot.astype(BF16), tri, (((2,), (0,)), ((), ())), preferred_element_type=F32)
    totals = inside[:, :, -1]
    before = jnp.cumsum(totals, axis=1) - totals
    rank = jnp.where(hot, inside + before[:, :, None] - 1.0, 0.0)
    place = jnp.sum(rank, axis=0).reshape(slots).astype(jnp.int32)
    flat = jnp.where(keep, owner * capacity + place, -1)
    code = pair_user * items + pair_item + 1
    spots = jnp.arange(4 * capacity, dtype=jnp.int32)
    return jnp.sum(jnp.where(flat[None, :] == spots[:, None], code[None, :], 0), axis=1).reshape(4, capacity)


def body(user_table, item_table, pair_user, pair_item, pair_owner, pair_count):
    users, width = user_table.shape
    items = item_table.shape[0]
    slots = pair_user.shape[0]
    total = float(slots * 128)
    core, x = lax.axis_index("core"), lax.axis_index("x")
    flag = core.reshape(1)

    codes = slot_lists(pair_user, pair_item, pair_owner, pair_count, items)
    named = codes > 0
    want = jnp.stack([jnp.where(named, (codes - 1) // items, -1), jnp.where(named, (codes - 1) % items, 0)], 1)
    got = lax.all_to_all(want, "x", 0, 0, tiled=True)
    lists = jnp.concatenate([lax.dynamic_slice_in_dim(got, (x + k) % 4, 1, 0) for k in (0, 3, 1, 2)], 0)
    rows, cols = lists[:, 0].reshape(-1), lists[:, 1].reshape(-1)

    user_table_sent, want = lax.optimization_barrier((user_table, want))
    left, right = shift(user_table_sent, "x", 1), shift(user_table_sent, "x", -1)
    far_a, far_b = shift(left[:users // 2], "x", 1), shift(right[users // 2:], "x", -1)

    keep = jnp.arange(slots, dtype=jnp.int32) < pair_count[0]
    user_counts = histogram(jnp.where(keep, pair_user, -1), users)
    item_counts = histogram(jnp.where(rows >= 0, cols, -1), items)
    keep_half, give_half = grams(flag, user_counts, item_counts, user_table, item_table)
    mine = keep_half + swap(give_half)
    mine = chip_scatter(mine.reshape(64, 72, NB))
    packed = chip_gather(mine).reshape(36 * NB, NB)

    spot = jnp.where(rows >= 0, rows, users)
    n = codes.shape[1]
    ct = cross(flag, spot[:n], cols[:n], item_table, (user_table,), (1,))
    ct = cross(flag, spot[n:3 * n], cols[n:3 * n], item_table, (left, right), (1, 1), ct)
    half, give = cross(flag, spot[3 * n:], cols[3 * n:], item_table, (far_a, far_b), (2,), ct, halves=True)
    half = half + swap(give)
    ct = chip_scatter(half.reshape(64, 8, width))

    mine = chol(packed, 1.0 / total)
    other = swap(mine)
    r_user, left = thin(flag, ct, mine, other, 0, float(total) ** -0.5)
    left = lax.all_to_all(left, CORE_FIRST, 0, 0, tiled=True).reshape(width, NB)
    r_item, whitened = thin(flag, left, mine, other, 1)
    return (r_user, r_item, whitened)


def solution(mesh):
    fine = Mesh(mesh.devices.reshape(4, 4, 2, 4), ALL)
    placed = (P(ALL, None), P("x", None), P(ALL), P(ALL), P(ALL), P(ALL))

    return jax.shard_map(
        body,
        mesh=fine,
        in_specs=placed,
        out_specs=(P(), P(), P(ALL, None)),
        check_vma=False,
    )
```

```python
import functools

import jax
import jax.numpy as jnp
from jax import lax
from jax.experimental import pallas as pl
from jax.experimental.pallas import tpu as pltpu
from jax.sharding import Mesh, PartitionSpec as P


N = 1024
NB = 128
KB = N // NB
SUB = 32
CHUNK = 512
SLOTS = 1024
HI = lax.Precision.HIGHEST
F32 = jnp.float32
BF16 = jnp.bfloat16
PACKED = 36 * NB
ALL = ("y", "z", "core", "x")
PAIRS_OF = [(i, j) for i in range(KB) for j in range(i, KB)]
START = {ij: NB * n for n, ij in enumerate(PAIRS_OF)}


def row_of(v, t):
    return jnp.broadcast_to(v[t:t + 1, :], v.shape)


def lane_of(v, c):
    return jnp.broadcast_to(v[:, c:c + 1], (8, NB))


def dot(a, b, ca, cb):
    return lax.dot_general(a, b, (((ca,), (cb,)), ((), ())), precision=HI, preferred_element_type=F32)


def parts(a):
    h = a.astype(BF16)
    rest = a - h.astype(F32)
    m = rest.astype(BF16)
    return h, m, (rest - m.astype(F32)).astype(BF16)


def stacks(a):
    h, m, l = parts(a)
    return jnp.concatenate([h, h, m, m, h, l], 0), jnp.concatenate([h, m, h, m, l, h], 0)


def tdot(a, b):
    return lax.dot_general(a, b, (((0,), (0,)), ((), ())), preferred_element_type=F32)


def factor(a, tmp):
    sub = lax.broadcasted_iota(jnp.int32, (8, NB), 0)
    groups = SUB // 8
    for s in range(NB // SUB):
        lo = SUB * s
        left = [a[lo + 8 * g:lo + 8 * g + 8, :NB] for g in range(groups)]
        right = [a[lo + 8 * g:lo + 8 * g + 8, NB:] for g in range(groups)]
        for g in range(groups):
            base = lo + 8 * g
            cols = [lane_of(left[g], base + t) for t in range(8)]
            for t in range(8):
                tmp[8 * t:8 * t + 8, :] = cols[t]
            ent = {(u, t): tmp[pl.ds(8 * t + u, 8, stride=0), :] for t in range(8) for u in range(t, 8)}
            fac, inv = {}, []
            for t in range(8):
                ri = lax.rsqrt(ent[t, t])
                inv.append(ri)
                for u in range(t + 1, 8):
                    fac[t, u] = ent[u, t] * ri
                for v in range(t + 1, 8):
                    for u in range(v, 8):
                        ent[u, v] = ent[u, v] - fac[t, u] * fac[t, v]
            rows_l, rows_r = [], []
            for t in range(8):
                pl_, pr_ = row_of(left[g], t), row_of(right[g], t)
                for k in range(t):
                    pl_ = pl_ - fac[k, t] * rows_l[k]
                    pr_ = pr_ - fac[k, t] * rows_r[k]
                rows_l.append(pl_ * inv[t])
                rows_r.append(pr_ * inv[t])
            for h in range(g + 1, groups):
                hc = [lane_of(left[h], base + t) for t in range(8)]
                for t in range(8):
                    ht = hc[t] * inv[t]
                    for u in range(t + 1, 8):
                        hc[u] = hc[u] - ht * fac[t, u]
                    left[h] = left[h] - ht * rows_l[t]
                    right[h] = right[h] - ht * rows_r[t]
            out_l, out_r = rows_l[0], rows_r[0]
            for t in range(1, 8):
                out_l = jnp.where(sub == t, rows_l[t], out_l)
                out_r = jnp.where(sub == t, rows_r[t], out_r)
            a[base:base + 8, :NB] = out_l
            a[base:base + 8, NB:] = out_r
        hi = lo + SUB
        if hi < NB:
            got = a[lo:hi, :]
            sa, sb = stacks(got)
            a[hi:, :] = a[hi:, :] - tdot(sa[:, hi:NB], sb)


def chol_kernel(scale, g_ref, out_ref, gp, r, a, tmp, got):
    row = lax.broadcasted_iota(jnp.int32, (NB, NB), 0)
    col = lax.broadcasted_iota(jnp.int32, (NB, NB), 1)
    eye = (row == col).astype(F32)

    def fetch(i):
        rows = pl.ds(START[i, i], NB * (KB - i))
        return pltpu.make_async_copy(g_ref.at[rows, :], gp.at[rows, :], got.at[i])

    for i in range(KB):
        fetch(i).start()
    for i in range(KB):
        fetch(i).wait()
        for j in range(i, KB):
            r[NB * i:NB * (i + 1), NB * j:NB * (j + 1)] = gp[START[i, j]:START[i, j] + NB, :] * scale

    def step(k, _):
        at = pl.multiple_of(k * NB, NB)
        here = pl.ds(at, NB)
        a[:, :NB] = r[here, here]
        a[:, NB:] = eye
        factor(a, tmp)
        out_ref[pl.ds(PACKED + at, NB), :] = a[:, NB:]
        r[here, here] = jnp.where(col >= row, a[:, :NB], 0.0)
        for s in range(KB - 1):
            @pl.when(k == s)
            def _(s=s):
                lo = NB * (s + 1)
                panel = dot(a[:, NB:], r[NB * s:lo, lo:], 1, 0)
                r[NB * s:lo, lo:] = panel
                sa, sb = stacks(panel)
                for i in range(lo, N, 256):
                    n = min(256, N - i)
                    r[i:i + n, i:] = r[i:i + n, i:] - tdot(sa[:, i - lo:i - lo + n], sb[:, i - lo:])
        return 0

    lax.fori_loop(0, KB, step, 0)
    for i, j in PAIRS_OF:
        out_ref[START[i, j]:START[i, j] + NB, :] = r[NB * i:NB * (i + 1), NB * j:NB * (j + 1)]


VM = pl.BlockSpec(memory_space=pltpu.VMEM)
HBM = pl.BlockSpec(memory_space=pltpu.HBM)
SM = pl.BlockSpec(memory_space=pltpu.SMEM)
PARAMS = pltpu.CompilerParams(vmem_limit_bytes=28 << 20)


def chol(packed, scale):
    return pl.pallas_call(
        functools.partial(chol_kernel, scale),
        out_shape=jax.ShapeDtypeStruct((PACKED + N, NB), F32),
        in_specs=[HBM],
        out_specs=VM,
        scratch_shapes=[
            pltpu.VMEM((PACKED, NB), F32),
            pltpu.VMEM((N, N), F32),
            pltpu.VMEM((NB, 2 * NB), F32),
            pltpu.VMEM((8 * 8, NB), F32),
            pltpu.SemaphoreType.DMA((KB,)),
        ],
        compiler_params=pltpu.CompilerParams(vmem_limit_bytes=60 << 20),
        cost_estimate=pl.CostEstimate(flops=1 << 33, bytes_accessed=8 << 20, transcendentals=0),
        name="chol",
    )(packed)


def small_dot(y, b, cb):
    low = y - y.astype(BF16).astype(F32)
    tail = low - low.astype(BF16).astype(F32)
    rows = jnp.concatenate([y, low, tail, jnp.zeros_like(y)], 0).astype(BF16)
    p, q, t = [lax.dot_general(rows, part, (((1,), (cb,)), ((), ())), preferred_element_type=F32) for part in parts(b)]
    return p[:8] + ((p[8:16] + q[:8]) + (p[16:24] + q[8:16] + t[:8]))


def place(m):
    core, chip, x = m // 64, m // 4 % 16, m % 4
    return (chip * 2 + core) * 4 + x


def thin_kernel(core_ref, y_ref, mine_ref, other_ref, r_ref, out_ref, rp, r, w, y, got, left, *, maker, scale):
    def rows(k):
        return pl.ds(START[k, k], NB * (KB - k))

    def fetch(src, k):
        return pltpu.make_async_copy(src.at[rows(k), :], rp.at[rows(k), :], got.at[k])

    def inverses(src):
        return pltpu.make_async_copy(src.at[pl.ds(PACKED, N), :], w, got.at[KB])

    def leave(k):
        block = pl.ds(k * NB, NB)
        return pltpu.make_async_copy(r.at[block, :], r_ref.at[block, :], left.at[k])

    def load(src):
        inverses(src).start()
        for k in range(KB):
            fetch(src, k).start()

    pl.when(core_ref[0] == maker)(lambda: load(mine_ref))
    pl.when(core_ref[0] != maker)(lambda: load(other_ref))
    if maker:
        for k in range(KB):
            y[:, NB * k:NB * (k + 1)] = jnp.transpose(y_ref[NB * k:NB * (k + 1), :])[:8, :]
    else:
        y[...] = y_ref[...] * scale
    inverses(mine_ref).wait()
    for k in range(KB):
        lo, hi = k * NB, (k + 1) * NB
        yk = small_dot(y[:, lo:hi], w[lo:hi, :], 1)
        if maker:
            out_ref[:, lo:hi] = yk
        else:
            for m in range(128):
                at = place(m) * 8 - lo
                if 0 <= at < NB:
                    out_ref[m, :, :] = pltpu.roll(yk, (NB - at) % NB, 1) if at else yk
        fetch(mine_ref, k).wait()
        blocks = [rp[START[k, j]:START[k, j] + NB, :] for j in range(k, KB)]
        if hi < N:
            y[:, hi:] = y[:, hi:] - small_dot(yk, jnp.concatenate(blocks[1:], 1), 0)
            r[hi:, lo:hi] = jnp.zeros((N - hi, NB), F32)
        for j in range(k, KB):
            r[lo:hi, NB * j:NB * (j + 1)] = blocks[j - k]
        leave(k).start()
    for k in range(KB):
        leave(k).wait()


def thin(core, y, mine, other, maker, scale=1.0):
    out = (8, N) if maker else (128, 8, NB)
    return pl.pallas_call(
        functools.partial(thin_kernel, maker=maker, scale=scale),
        out_shape=(jax.ShapeDtypeStruct((N, N), F32), jax.ShapeDtypeStruct(out, F32)),
        in_specs=[SM, VM, HBM, HBM],
        out_specs=(HBM, VM),
        scratch_shapes=[
            pltpu.VMEM((PACKED, NB), F32),
            pltpu.VMEM((N, N), F32),
            pltpu.VMEM((N, NB), F32),
            pltpu.VMEM((8, N), F32),
            pltpu.SemaphoreType.DMA((KB + 1,)),
            pltpu.SemaphoreType.DMA((KB,)),
        ],
        compiler_params=pltpu.CompilerParams(vmem_limit_bytes=60 << 20),
        name="thin",
    )(core, y, mine, other)


def gram_kernel(core_ref, cu_ref, ci_ref, u_ref, i_ref, keep_ref, give_ref, counts, acc):
    eye = lax.broadcasted_iota(jnp.int32, (NB, NB), 0) == lax.broadcasted_iota(jnp.int32, (NB, NB), 1)

    def put(ref):
        for i, j in PAIRS_OF:
            at = START[i, j]
            ref[at:at + NB, :] = acc[NB * i:NB * (i + 1), NB * j:NB * (j + 1)]

    for maker, table in enumerate((u_ref, i_ref)):
        rows = table.shape[0]
        counts[:rows // NB, :] = ci_ref[...] if maker else cu_ref[...]
        acc[...] = jnp.zeros((N, N), F32)

        def chunk(c):
            times = [jnp.sum(jnp.where(eye, counts[pl.ds(c * (CHUNK // NB) + b, 1), :], 0.0), axis=1, keepdims=True) for b in range(CHUNK // NB)]
            t = table[pl.ds(pl.multiple_of(c * CHUNK, CHUNK), CHUNK), :]
            weighted = t.astype(F32) * jnp.concatenate(times, 0)
            high = weighted.astype(BF16)
            both = jnp.concatenate([high, (weighted - high.astype(F32)).astype(BF16)], 0)
            tt = jnp.concatenate([t, t], 0)
            for i in range(0, N, 256):
                acc[i:i + 256, i:] = acc[i:i + 256, i:] + tdot(tt[:, i:i + 256], both[:, i:])

        def chunks(c, _):
            for k in range(1 + maker):
                chunk(c * (1 + maker) + k)
            return 0

        lax.fori_loop(0, 2, chunks, 0)
        pl.when(core_ref[0] == maker)(lambda: put(keep_ref))
        pl.when(core_ref[0] != maker)(lambda: put(give_ref))


def grams(core, user_counts, item_counts, user_table, item_table):
    packed = jax.ShapeDtypeStruct((36 * NB, NB), F32)
    return pl.pallas_call(
        gram_kernel,
        out_shape=(packed, packed),
        in_specs=[SM, VM, VM, VM, VM],
        out_specs=(VM, VM),
        scratch_shapes=[pltpu.VMEM((16, NB), F32), pltpu.VMEM((N, N), F32)],
        compiler_params=PARAMS,
        cost_estimate=pl.CostEstimate(flops=1 << 33, bytes_accessed=10 << 20, transcendentals=0),
        name="grams",
    )(core, user_counts, item_counts, user_table, item_table)


def spread_rows(src, dst):
    def tile(r, _):
        at = pl.multiple_of(r * 16, 16)
        for c in range(KB):
            dst[pl.ds(at * KB + c, 16, stride=KB), :] = src[pl.ds(at, 16), NB * c:NB * (c + 1)].astype(F32)
        return 0

    lax.fori_loop(0, src.shape[0] // 16, tile, 0)


def gather_rows(src, dst):
    def tile(r, _):
        at = pl.multiple_of(r * 16, 16)
        for c in range(KB):
            dst[pl.ds(at, 16), NB * c:NB * (c + 1)] = src[pl.ds(at * KB + c, 16, stride=KB), :].astype(BF16)
        return 0

    lax.fori_loop(0, dst.shape[0] // 16, tile, 0)


def cross_kernel(core_ref, at_ref, col_ref, i_ref, *refs, groups, first, add, halves):
    count = sum(groups)
    tables, refs = refs[:count], refs[count:]
    if add:
        old_ref, refs = refs[0], refs[1:]
    outs, refs = refs[:1 + halves], refs[1 + halves:]
    ib, ub, uf, itf, pu, pi, panel, panel_i, acc, got_i, got_u, got_old, left = refs
    last = len(groups) - 1
    spots = [(g, t) for g, n in enumerate(groups) for t in range(n)]

    def item_copy():
        return pltpu.make_async_copy(i_ref, ib, got_i)

    def old_copy():
        return pltpu.make_async_copy(old_ref, acc, got_old)

    def table_copy(n):
        g, t = spots[n]
        rows = tables[n].shape[0]
        return pltpu.make_async_copy(tables[n], ub.at[g, pl.ds(t * rows, rows), :], got_u.at[n])

    def leave(b, ref, to):
        rows = pl.ds(pl.multiple_of(b * 256, 256), 256)
        return pltpu.make_async_copy(acc.at[rows, :], ref.at[pl.ds(pl.multiple_of(to * 256, 256), 256), :], left.at[b])

    item_copy().start()
    for n in range(count):
        table_copy(n).start()
    if add:
        old_copy().start()
    item_copy().wait()
    spread_rows(ib, itf)
    uf[N * KB:, :] = jnp.zeros((KB, NB), F32)

    def group(g, _):
        for j in range(len(groups)):
            @pl.when(g == j)
            def _(j=j):
                for n in range(count):
                    if spots[n][0] == j:
                        table_copy(n).wait()
                spread_rows(ub.at[j], uf)

        base = core_ref[1 + first + g] * SLOTS

        def move(b, _):
            for k in range(8):
                s = b * 8 + k
                u = at_ref[base + s]
                i = col_ref[base + s]
                to = pl.ds(pl.multiple_of(s * KB, KB), KB)
                pu[to, :] = uf[pl.ds(pl.multiple_of(u * KB, KB), KB), :]
                pi[to, :] = itf[pl.ds(pl.multiple_of(i * KB, KB), KB), :]
            return 0

        lax.fori_loop(0, SLOTS // 8, move, 0)
        gather_rows(pu, panel)
        gather_rows(pi, panel_i)
        if add:
            @pl.when(g == 0)
            def _():
                old_copy().wait()

        def block(b, _):
            rows = pl.ds(pl.multiple_of(b * 256, 256), 256)
            got = tdot(panel_i[:, rows], panel[...])
            if add:
                acc[rows, :] = acc[rows, :] + got
            else:
                acc[rows, :] = got

            @pl.when(g == last)
            def _():
                if halves:
                    mine = b // 2 == core_ref[0]
                    pl.when(mine)(lambda: leave(b, outs[0], b % 2).start())
                    pl.when(jnp.logical_not(mine))(lambda: leave(b, outs[1], b % 2).start())
                else:
                    leave(b, outs[0], b).start()

            return 0

        lax.fori_loop(0, N // 256, block, 0)
        return 0

    lax.fori_loop(0, len(groups), group, 0)
    for b in range(N // 256):
        leave(b, outs[0], 0).wait()


def cross(flag, at, cols, item_table, tables, groups, first, old=None, halves=False):
    assert old is not None or len(groups) == 1
    items = item_table.shape[0]
    more = () if old is None else (old,)
    full, half = jax.ShapeDtypeStruct((N, N), F32), jax.ShapeDtypeStruct((N // 2, N), F32)
    return pl.pallas_call(
        functools.partial(cross_kernel, groups=groups, first=first, add=old is not None, halves=halves),
        out_shape=(half, half) if halves else full,
        in_specs=[SM, SM, SM] + [HBM] * (1 + len(tables) + len(more)),
        out_specs=(HBM, HBM) if halves else HBM,
        scratch_shapes=[
            pltpu.VMEM((items, N), BF16),
            pltpu.VMEM((len(groups), N, N), BF16),
            pltpu.VMEM(((N + 1) * KB, NB), F32),
            pltpu.VMEM((items * KB, NB), F32),
            pltpu.VMEM((SLOTS * KB, NB), F32),
            pltpu.VMEM((SLOTS * KB, NB), F32),
            pltpu.VMEM((SLOTS, N), BF16),
            pltpu.VMEM((SLOTS, N), BF16),
            pltpu.VMEM((N, N), F32),
            pltpu.SemaphoreType.DMA,
            pltpu.SemaphoreType.DMA((len(tables),)),
            pltpu.SemaphoreType.DMA,
            pltpu.SemaphoreType.DMA((N // 256,)),
        ],
        compiler_params=pltpu.CompilerParams(vmem_limit_bytes=60 << 20),
        cost_estimate=pl.CostEstimate(flops=len(groups) << 32, bytes_accessed=12 << 20, transcendentals=0),
        name="cross",
    )(flag, at, cols, item_table, *tables, *more)


CHIPS = ("y", "z", "x")
CORE_FIRST = ("core", "y", "z", "x")


def swap(b):
    return lax.ppermute(b, "core", [(0, 1), (1, 0)])


def histogram(key, bins):
    hot = (key[None, :] // NB == jnp.arange(bins // NB, dtype=jnp.int32)[:, None]) & (key >= 0)[None, :]
    lane = key[:, None] % NB == jnp.arange(NB, dtype=jnp.int32)[None, :]
    return lax.dot_general(hot.astype(BF16), lane.astype(BF16), (((1,), (0,)), ((), ())), preferred_element_type=F32)


def chip_scatter(b):
    return jnp.sum(lax.all_to_all(b, CHIPS, 0, 0, tiled=True), 0)


def chip_gather(b):
    return lax.all_to_all(jnp.broadcast_to(b[None], (64,) + b.shape), CHIPS, 0, 0, tiled=True)


def ring(k):
    return [(i, (i + k) % 4) for i in range(4)]


def shift(b, axis, k):
    return lax.ppermute(b, axis, ring(k % 4))


def slot_lists(pair_user, pair_item, pair_owner, pair_count, items):
    slots = pair_owner.shape[0]
    capacity = slots // 2
    keep = jnp.arange(slots, dtype=jnp.int32) < pair_count[0]
    owner = jnp.where(keep, pair_owner, -1)
    hot = (owner[None, :] == jnp.arange(4, dtype=jnp.int32)[:, None]).reshape(4, slots // NB, NB)
    tri = (jnp.arange(NB)[:, None] <= jnp.arange(NB)[None, :]).astype(BF16)
    inside = lax.dot_general(hot.astype(BF16), tri, (((2,), (0,)), ((), ())), preferred_element_type=F32)
    totals = inside[:, :, -1]
    before = jnp.cumsum(totals, axis=1) - totals
    rank = jnp.where(hot, inside + before[:, :, None] - 1.0, 0.0)
    place = jnp.sum(rank, axis=0).reshape(slots).astype(jnp.int32)
    flat = jnp.where(keep, owner * capacity + place, -1)
    code = pair_user * items + pair_item + 1
    spots = jnp.arange(4 * capacity, dtype=jnp.int32)
    return jnp.sum(jnp.where(flat[None, :] == spots[:, None], code[None, :], 0), axis=1).reshape(4, capacity)


def body(user_table, item_table, pair_user, pair_item, pair_owner, pair_count):
    users, width = user_table.shape
    items = item_table.shape[0]
    slots = pair_user.shape[0]
    total = float(slots * 128)
    core, x = lax.axis_index("core"), lax.axis_index("x")
    flag = jnp.stack([core] + [(x + k) % 4 for k in (0, 3, 1, 2)])

    codes = slot_lists(pair_user, pair_item, pair_owner, pair_count, items)
    named = codes > 0
    want = jnp.stack([jnp.where(named, (codes - 1) // items, -1), jnp.where(named, (codes - 1) % items, 0)], 1)
    got = lax.all_to_all(want, "x", 0, 0, tiled=True)
    rows, cols = got[:, 0].reshape(-1), got[:, 1].reshape(-1)

    user_table_sent, want = lax.optimization_barrier((user_table, want))
    left, right = shift(user_table_sent, "x", 1), shift(user_table_sent, "x", -1)
    far_a, far_b = shift(left[:users // 2], "x", 1), shift(right[users // 2:], "x", -1)

    keep = jnp.arange(slots, dtype=jnp.int32) < pair_count[0]
    user_counts = histogram(jnp.where(keep, pair_user, -1), users)
    item_counts = histogram(jnp.where(rows >= 0, cols, -1), items)
    keep_half, give_half = grams(flag, user_counts, item_counts, user_table, item_table)
    mine = keep_half + swap(give_half)
    mine = chip_scatter(mine.reshape(64, 72, NB))
    packed = chip_gather(mine).reshape(36 * NB, NB)

    spot = jnp.where(rows >= 0, rows, users)
    ct = cross(flag, spot, cols, item_table, (user_table,), (1,), 0)
    ct = cross(flag, spot, cols, item_table, (left, right), (1, 1), 1, ct)
    half, give = cross(flag, spot, cols, item_table, (far_a, far_b), (2,), 3, ct, halves=True)
    half = half + swap(give)
    ct = chip_scatter(half.reshape(64, 8, width))

    mine = chol(packed, 1.0 / total)
    other = swap(mine)
    r_user, left = thin(flag, ct, mine, other, 0, float(total) ** -0.5)
    left = lax.all_to_all(left, CORE_FIRST, 0, 0, tiled=True).reshape(width, NB)
    r_item, whitened = thin(flag, left, mine, other, 1)
    return (r_user, r_item, whitened)


def solution(mesh):
    fine = Mesh(mesh.devices.reshape(4, 4, 2, 4), ALL)
    placed = (P(ALL, None), P("x", None), P(ALL), P(ALL), P(ALL), P(ALL))

    return jax.shard_map(
        body,
        mesh=fine,
        in_specs=placed,
        out_specs=(P(), P(), P(ALL, None)),
        check_vma=False,
    )
```

```python
import functools

import jax
import jax.numpy as jnp
from jax import lax
from jax.experimental import pallas as pl
from jax.experimental.pallas import tpu as pltpu
from jax.sharding import Mesh, PartitionSpec as P


N = 1024
NB = 128
KB = N // NB
SUB = 32
CHUNK = 512
SLOTS = 1024
HI = lax.Precision.HIGHEST
F32 = jnp.float32
BF16 = jnp.bfloat16
PACKED = 36 * NB
ALL = ("y", "z", "core", "x")
PAIRS_OF = [(i, j) for i in range(KB) for j in range(i, KB)]
START = {ij: NB * n for n, ij in enumerate(PAIRS_OF)}


def row_of(v, t):
    return jnp.broadcast_to(v[t:t + 1, :], v.shape)


def lane_of(v, c):
    return jnp.broadcast_to(v[:, c:c + 1], (8, NB))


def dot(a, b, ca, cb):
    return lax.dot_general(a, b, (((ca,), (cb,)), ((), ())), precision=HI, preferred_element_type=F32)


def parts(a):
    h = a.astype(BF16)
    rest = a - h.astype(F32)
    m = rest.astype(BF16)
    return h, m, (rest - m.astype(F32)).astype(BF16)


def stacks(a):
    h, m, l = parts(a)
    return jnp.concatenate([h, h, m, m, h, l], 0), jnp.concatenate([h, m, h, m, l, h], 0)


def tdot(a, b):
    return lax.dot_general(a, b, (((0,), (0,)), ((), ())), preferred_element_type=F32)


def factor(a, tmp):
    sub = lax.broadcasted_iota(jnp.int32, (8, NB), 0)
    groups = SUB // 8
    for s in range(NB // SUB):
        lo = SUB * s
        left = [a[lo + 8 * g:lo + 8 * g + 8, :NB] for g in range(groups)]
        right = [a[lo + 8 * g:lo + 8 * g + 8, NB:] for g in range(groups)]
        for g in range(groups):
            base = lo + 8 * g
            cols = [lane_of(left[g], base + t) for t in range(8)]
            for t in range(8):
                tmp[8 * t:8 * t + 8, :] = cols[t]
            ent = {(u, t): tmp[pl.ds(8 * t + u, 8, stride=0), :] for t in range(8) for u in range(t, 8)}
            fac, inv = {}, []
            for t in range(8):
                ri = lax.rsqrt(ent[t, t])
                inv.append(ri)
                for u in range(t + 1, 8):
                    fac[t, u] = ent[u, t] * ri
                for v in range(t + 1, 8):
                    for u in range(v, 8):
                        ent[u, v] = ent[u, v] - fac[t, u] * fac[t, v]
            rows_l, rows_r = [], []
            for t in range(8):
                pl_, pr_ = row_of(left[g], t), row_of(right[g], t)
                for k in range(t):
                    pl_ = pl_ - fac[k, t] * rows_l[k]
                    pr_ = pr_ - fac[k, t] * rows_r[k]
                rows_l.append(pl_ * inv[t])
                rows_r.append(pr_ * inv[t])
            for h in range(g + 1, groups):
                hc = [lane_of(left[h], base + t) for t in range(8)]
                for t in range(8):
                    ht = hc[t] * inv[t]
                    for u in range(t + 1, 8):
                        hc[u] = hc[u] - ht * fac[t, u]
                    left[h] = left[h] - ht * rows_l[t]
                    right[h] = right[h] - ht * rows_r[t]
            out_l, out_r = rows_l[0], rows_r[0]
            for t in range(1, 8):
                out_l = jnp.where(sub == t, rows_l[t], out_l)
                out_r = jnp.where(sub == t, rows_r[t], out_r)
            a[base:base + 8, :NB] = out_l
            a[base:base + 8, NB:] = out_r
        hi = lo + SUB
        if hi < NB:
            got = a[lo:hi, :]
            sa, sb = stacks(got)
            a[hi:, :] = a[hi:, :] - tdot(sa[:, hi:NB], sb)


def chol_kernel(scale, g_ref, out_ref, gp, r, a, tmp, got):
    row = lax.broadcasted_iota(jnp.int32, (NB, NB), 0)
    col = lax.broadcasted_iota(jnp.int32, (NB, NB), 1)
    eye = (row == col).astype(F32)

    def fetch(i):
        rows = pl.ds(START[i, i], NB * (KB - i))
        return pltpu.make_async_copy(g_ref.at[rows, :], gp.at[rows, :], got.at[i])

    for i in range(KB):
        fetch(i).start()
    for i in range(KB):
        fetch(i).wait()
        for j in range(i, KB):
            r[NB * i:NB * (i + 1), NB * j:NB * (j + 1)] = gp[START[i, j]:START[i, j] + NB, :] * scale

    def step(k, _):
        at = pl.multiple_of(k * NB, NB)
        here = pl.ds(at, NB)
        a[:, :NB] = r[here, here]
        a[:, NB:] = eye
        factor(a, tmp)
        out_ref[pl.ds(PACKED + at, NB), :] = a[:, NB:]
        r[here, here] = jnp.where(col >= row, a[:, :NB], 0.0)
        for s in range(KB - 1):
            @pl.when(k == s)
            def _(s=s):
                lo = NB * (s + 1)
                panel = dot(a[:, NB:], r[NB * s:lo, lo:], 1, 0)
                r[NB * s:lo, lo:] = panel
                sa, sb = stacks(panel)
                for i in range(lo, N, 256):
                    n = min(256, N - i)
                    r[i:i + n, i:] = r[i:i + n, i:] - tdot(sa[:, i - lo:i - lo + n], sb[:, i - lo:])
        return 0

    lax.fori_loop(0, KB, step, 0)
    for i, j in PAIRS_OF:
        out_ref[START[i, j]:START[i, j] + NB, :] = r[NB * i:NB * (i + 1), NB * j:NB * (j + 1)]


VM = pl.BlockSpec(memory_space=pltpu.VMEM)
HBM = pl.BlockSpec(memory_space=pltpu.HBM)
SM = pl.BlockSpec(memory_space=pltpu.SMEM)
PARAMS = pltpu.CompilerParams(vmem_limit_bytes=28 << 20)


def chol(packed, scale):
    return pl.pallas_call(
        functools.partial(chol_kernel, scale),
        out_shape=jax.ShapeDtypeStruct((PACKED + N, NB), F32),
        in_specs=[HBM],
        out_specs=VM,
        scratch_shapes=[
            pltpu.VMEM((PACKED, NB), F32),
            pltpu.VMEM((N, N), F32),
            pltpu.VMEM((NB, 2 * NB), F32),
            pltpu.VMEM((8 * 8, NB), F32),
            pltpu.SemaphoreType.DMA((KB,)),
        ],
        compiler_params=pltpu.CompilerParams(vmem_limit_bytes=60 << 20),
        cost_estimate=pl.CostEstimate(flops=1 << 33, bytes_accessed=8 << 20, transcendentals=0),
        name="chol",
    )(packed)


def small_dot(y, b, cb):
    low = y - y.astype(BF16).astype(F32)
    tail = low - low.astype(BF16).astype(F32)
    rows = jnp.concatenate([y, low, tail, jnp.zeros_like(y)], 0).astype(BF16)
    p, q, t = [lax.dot_general(rows, part, (((1,), (cb,)), ((), ())), preferred_element_type=F32) for part in parts(b)]
    return p[:8] + ((p[8:16] + q[:8]) + (p[16:24] + q[8:16] + t[:8]))


def place(m):
    core, chip, x = m // 64, m // 4 % 16, m % 4
    return (chip * 2 + core) * 4 + x


def thin_kernel(core_ref, y_ref, mine_ref, other_ref, r_ref, out_ref, rp, r, w, y, got, left, *, maker, scale):
    def rows(k):
        return pl.ds(START[k, k], NB * (KB - k))

    def fetch(src, k):
        return pltpu.make_async_copy(src.at[rows(k), :], rp.at[rows(k), :], got.at[k])

    def inverses(src):
        return pltpu.make_async_copy(src.at[pl.ds(PACKED, N), :], w, got.at[KB])

    def leave(k):
        block = pl.ds(k * NB, NB)
        return pltpu.make_async_copy(r.at[block, :], r_ref.at[block, :], left.at[k])

    def load(src):
        inverses(src).start()
        for k in range(KB):
            fetch(src, k).start()

    pl.when(core_ref[0] == maker)(lambda: load(mine_ref))
    pl.when(core_ref[0] != maker)(lambda: load(other_ref))
    if maker:
        for k in range(KB):
            y[:, NB * k:NB * (k + 1)] = jnp.transpose(y_ref[NB * k:NB * (k + 1), :])[:8, :]
    else:
        y[...] = y_ref[...] * scale
    inverses(mine_ref).wait()
    for k in range(KB):
        lo, hi = k * NB, (k + 1) * NB
        yk = small_dot(y[:, lo:hi], w[lo:hi, :], 1)
        if maker:
            out_ref[:, lo:hi] = yk
        else:
            for m in range(128):
                at = place(m) * 8 - lo
                if 0 <= at < NB:
                    out_ref[m, :, :] = pltpu.roll(yk, (NB - at) % NB, 1) if at else yk
        fetch(mine_ref, k).wait()
        blocks = [rp[START[k, j]:START[k, j] + NB, :] for j in range(k, KB)]
        if hi < N:
            y[:, hi:] = y[:, hi:] - small_dot(yk, jnp.concatenate(blocks[1:], 1), 0)
            r[hi:, lo:hi] = jnp.zeros((N - hi, NB), F32)
        for j in range(k, KB):
            r[lo:hi, NB * j:NB * (j + 1)] = blocks[j - k]
        leave(k).start()
    for k in range(KB):
        leave(k).wait()


def thin(core, y, mine, other, maker, scale=1.0):
    out = (8, N) if maker else (128, 8, NB)
    return pl.pallas_call(
        functools.partial(thin_kernel, maker=maker, scale=scale),
        out_shape=(jax.ShapeDtypeStruct((N, N), F32), jax.ShapeDtypeStruct(out, F32)),
        in_specs=[SM, VM, HBM, HBM],
        out_specs=(HBM, VM),
        scratch_shapes=[
            pltpu.VMEM((PACKED, NB), F32),
            pltpu.VMEM((N, N), F32),
            pltpu.VMEM((N, NB), F32),
            pltpu.VMEM((8, N), F32),
            pltpu.SemaphoreType.DMA((KB + 1,)),
            pltpu.SemaphoreType.DMA((KB,)),
        ],
        compiler_params=pltpu.CompilerParams(vmem_limit_bytes=60 << 20),
        name="thin",
    )(core, y, mine, other)


def gram_kernel(core_ref, cu_ref, ci_ref, u_ref, i_ref, keep_ref, give_ref, counts, acc, u_buf, i_buf, packs, got, left):
    eye = lax.broadcasted_iota(jnp.int32, (NB, NB), 0) == lax.broadcasted_iota(jnp.int32, (NB, NB), 1)

    def fetch(n):
        return pltpu.make_async_copy((u_ref, i_ref)[n], (u_buf, i_buf)[n], got.at[n])

    def leave(n, ref):
        return pltpu.make_async_copy(packs.at[n], ref, left.at[n])

    fetch(0).start()
    fetch(1).start()
    for maker, table in enumerate((u_buf, i_buf)):
        fetch(maker).wait()
        rows = table.shape[0]
        counts[:rows // NB, :] = ci_ref[...] if maker else cu_ref[...]
        acc[...] = jnp.zeros((N, N), F32)

        def chunk(c):
            times = [jnp.sum(jnp.where(eye, counts[pl.ds(c * (CHUNK // NB) + b, 1), :], 0.0), axis=1, keepdims=True) for b in range(CHUNK // NB)]
            t = table[pl.ds(pl.multiple_of(c * CHUNK, CHUNK), CHUNK), :]
            weighted = t.astype(F32) * jnp.concatenate(times, 0)
            high = weighted.astype(BF16)
            both = jnp.concatenate([high, (weighted - high.astype(F32)).astype(BF16)], 0)
            tt = jnp.concatenate([t, t], 0)
            for i in range(0, N, 256):
                acc[i:i + 256, i:] = acc[i:i + 256, i:] + tdot(tt[:, i:i + 256], both[:, i:])

        def chunks(c, _):
            for k in range(1 + maker):
                chunk(c * (1 + maker) + k)
            return 0

        lax.fori_loop(0, 2, chunks, 0)
        for i, j in PAIRS_OF:
            at = START[i, j]
            packs[maker, at:at + NB, :] = acc[NB * i:NB * (i + 1), NB * j:NB * (j + 1)]
        pl.when(core_ref[0] == maker)(lambda maker=maker: leave(maker, keep_ref).start())
        pl.when(core_ref[0] != maker)(lambda maker=maker: leave(maker, give_ref).start())
    for maker in range(2):
        leave(maker, keep_ref).wait()


def grams(core, user_counts, item_counts, user_table, item_table):
    packed = jax.ShapeDtypeStruct((36 * NB, NB), F32)
    return pl.pallas_call(
        gram_kernel,
        out_shape=(packed, packed),
        in_specs=[SM, VM, VM, HBM, HBM],
        out_specs=(HBM, HBM),
        scratch_shapes=[
            pltpu.VMEM((16, NB), F32),
            pltpu.VMEM((N, N), F32),
            pltpu.VMEM(user_table.shape, BF16),
            pltpu.VMEM(item_table.shape, BF16),
            pltpu.VMEM((2, PACKED, NB), F32),
            pltpu.SemaphoreType.DMA((2,)),
            pltpu.SemaphoreType.DMA((2,)),
        ],
        compiler_params=pltpu.CompilerParams(vmem_limit_bytes=60 << 20),
        cost_estimate=pl.CostEstimate(flops=1 << 33, bytes_accessed=10 << 20, transcendentals=0),
        name="grams",
    )(core, user_counts, item_counts, user_table, item_table)


def spread_rows(src, dst):
    def tile(r, _):
        at = pl.multiple_of(r * 16, 16)
        for c in range(KB):
            dst[pl.ds(at * KB + c, 16, stride=KB), :] = src[pl.ds(at, 16), NB * c:NB * (c + 1)].astype(F32)
        return 0

    lax.fori_loop(0, src.shape[0] // 16, tile, 0)


def gather_rows(src, dst):
    def tile(r, _):
        at = pl.multiple_of(r * 16, 16)
        for c in range(KB):
            dst[pl.ds(at, 16), NB * c:NB * (c + 1)] = src[pl.ds(at * KB + c, 16, stride=KB), :].astype(BF16)
        return 0

    lax.fori_loop(0, dst.shape[0] // 16, tile, 0)


def cross_kernel(core_ref, at_ref, col_ref, i_ref, *refs, groups, first, add, halves):
    count = sum(groups)
    tables, refs = refs[:count], refs[count:]
    if add:
        old_ref, refs = refs[0], refs[1:]
    outs, refs = refs[:1 + halves], refs[1 + halves:]
    ib, ub, uf, itf, pu, pi, panel, panel_i, acc, got_i, got_u, got_old, left = refs
    last = len(groups) - 1
    spots = [(g, t) for g, n in enumerate(groups) for t in range(n)]

    def item_copy():
        return pltpu.make_async_copy(i_ref, ib, got_i)

    def old_copy():
        return pltpu.make_async_copy(old_ref, acc, got_old)

    def table_copy(n):
        g, t = spots[n]
        rows = tables[n].shape[0]
        return pltpu.make_async_copy(tables[n], ub.at[g, pl.ds(t * rows, rows), :], got_u.at[n])

    def leave(b, ref, to):
        rows = pl.ds(pl.multiple_of(b * 256, 256), 256)
        return pltpu.make_async_copy(acc.at[rows, :], ref.at[pl.ds(pl.multiple_of(to * 256, 256), 256), :], left.at[b])

    item_copy().start()
    for n in range(count):
        table_copy(n).start()
    if add:
        old_copy().start()
    item_copy().wait()
    spread_rows(ib, itf)
    uf[N * KB:, :] = jnp.zeros((KB, NB), F32)

    def group(g, _):
        for j in range(len(groups)):
            @pl.when(g == j)
            def _(j=j):
                for n in range(count):
                    if spots[n][0] == j:
                        table_copy(n).wait()
                spread_rows(ub.at[j], uf)

        base = core_ref[1 + first + g] * SLOTS

        def move(b, _):
            for k in range(8):
                s = b * 8 + k
                u = at_ref[base + s]
                i = col_ref[base + s]
                to = pl.ds(pl.multiple_of(s * KB, KB), KB)
                pu[to, :] = uf[pl.ds(pl.multiple_of(u * KB, KB), KB), :]
                pi[to, :] = itf[pl.ds(pl.multiple_of(i * KB, KB), KB), :]
            return 0

        lax.fori_loop(0, SLOTS // 8, move, 0)
        gather_rows(pu, panel)
        gather_rows(pi, panel_i)
        if add:
            @pl.when(g == 0)
            def _():
                old_copy().wait()

        def block(b, _):
            rows = pl.ds(pl.multiple_of(b * 256, 256), 256)
            got = tdot(panel_i[:, rows], panel[...])
            if add:
                acc[rows, :] = acc[rows, :] + got
            else:
                acc[rows, :] = got

            @pl.when(g == last)
            def _():
                if halves:
                    mine = b // 2 == core_ref[0]
                    pl.when(mine)(lambda: leave(b, outs[0], b % 2).start())
                    pl.when(jnp.logical_not(mine))(lambda: leave(b, outs[1], b % 2).start())
                else:
                    leave(b, outs[0], b).start()

            return 0

        lax.fori_loop(0, N // 256, block, 0)
        return 0

    lax.fori_loop(0, len(groups), group, 0)
    for b in range(N // 256):
        leave(b, outs[0], 0).wait()


def cross(flag, at, cols, item_table, tables, groups, first, old=None, halves=False):
    assert old is not None or len(groups) == 1
    items = item_table.shape[0]
    more = () if old is None else (old,)
    full, half = jax.ShapeDtypeStruct((N, N), F32), jax.ShapeDtypeStruct((N // 2, N), F32)
    return pl.pallas_call(
        functools.partial(cross_kernel, groups=groups, first=first, add=old is not None, halves=halves),
        out_shape=(half, half) if halves else full,
        in_specs=[SM, SM, SM] + [HBM] * (1 + len(tables) + len(more)),
        out_specs=(HBM, HBM) if halves else HBM,
        scratch_shapes=[
            pltpu.VMEM((items, N), BF16),
            pltpu.VMEM((len(groups), N, N), BF16),
            pltpu.VMEM(((N + 1) * KB, NB), F32),
            pltpu.VMEM((items * KB, NB), F32),
            pltpu.VMEM((SLOTS * KB, NB), F32),
            pltpu.VMEM((SLOTS * KB, NB), F32),
            pltpu.VMEM((SLOTS, N), BF16),
            pltpu.VMEM((SLOTS, N), BF16),
            pltpu.VMEM((N, N), F32),
            pltpu.SemaphoreType.DMA,
            pltpu.SemaphoreType.DMA((len(tables),)),
            pltpu.SemaphoreType.DMA,
            pltpu.SemaphoreType.DMA((N // 256,)),
        ],
        compiler_params=pltpu.CompilerParams(vmem_limit_bytes=60 << 20),
        cost_estimate=pl.CostEstimate(flops=len(groups) << 32, bytes_accessed=12 << 20, transcendentals=0),
        name="cross",
    )(flag, at, cols, item_table, *tables, *more)


CHIPS = ("y", "z", "x")
CORE_FIRST = ("core", "y", "z", "x")


def swap(b):
    return lax.ppermute(b, "core", [(0, 1), (1, 0)])


def histogram(key, bins):
    hot = (key[None, :] // NB == jnp.arange(bins // NB, dtype=jnp.int32)[:, None]) & (key >= 0)[None, :]
    lane = key[:, None] % NB == jnp.arange(NB, dtype=jnp.int32)[None, :]
    return lax.dot_general(hot.astype(BF16), lane.astype(BF16), (((1,), (0,)), ((), ())), preferred_element_type=F32)


def chip_scatter(b):
    return jnp.sum(lax.all_to_all(b, CHIPS, 0, 0, tiled=True), 0)


def chip_gather(b):
    return lax.all_to_all(jnp.broadcast_to(b[None], (64,) + b.shape), CHIPS, 0, 0, tiled=True)


def ring(k):
    return [(i, (i + k) % 4) for i in range(4)]


def shift(b, axis, k):
    return lax.ppermute(b, axis, ring(k % 4))


def slot_lists(pair_user, pair_item, pair_owner, pair_count, items):
    slots = pair_owner.shape[0]
    capacity = slots // 2
    keep = jnp.arange(slots, dtype=jnp.int32) < pair_count[0]
    owner = jnp.where(keep, pair_owner, -1)
    hot = (owner[None, :] == jnp.arange(4, dtype=jnp.int32)[:, None]).reshape(4, slots // NB, NB)
    tri = (jnp.arange(NB)[:, None] <= jnp.arange(NB)[None, :]).astype(BF16)
    inside = lax.dot_general(hot.astype(BF16), tri, (((2,), (0,)), ((), ())), preferred_element_type=F32)
    totals = inside[:, :, -1]
    before = jnp.cumsum(totals, axis=1) - totals
    rank = jnp.where(hot, inside + before[:, :, None] - 1.0, 0.0)
    place = jnp.sum(rank, axis=0).reshape(slots).astype(jnp.int32)
    flat = jnp.where(keep, owner * capacity + place, -1)
    code = pair_user * items + pair_item + 1
    spots = jnp.arange(4 * capacity, dtype=jnp.int32)
    return jnp.sum(jnp.where(flat[None, :] == spots[:, None], code[None, :], 0), axis=1).reshape(4, capacity)


def body(user_table, item_table, pair_user, pair_item, pair_owner, pair_count):
    users, width = user_table.shape
    items = item_table.shape[0]
    slots = pair_user.shape[0]
    total = float(slots * 128)
    core, x = lax.axis_index("core"), lax.axis_index("x")
    flag = jnp.stack([core] + [(x + k) % 4 for k in (0, 3, 1, 2)])

    codes = slot_lists(pair_user, pair_item, pair_owner, pair_count, items)
    named = codes > 0
    want = jnp.stack([jnp.where(named, (codes - 1) // items, -1), jnp.where(named, (codes - 1) % items, 0)], 1)
    got = lax.all_to_all(want, "x", 0, 0, tiled=True)
    rows, cols = got[:, 0].reshape(-1), got[:, 1].reshape(-1)

    user_table_sent, want = lax.optimization_barrier((user_table, want))
    left, right = shift(user_table_sent, "x", 1), shift(user_table_sent, "x", -1)
    far_a, far_b = shift(left[:users // 2], "x", 1), shift(right[users // 2:], "x", -1)

    keep = jnp.arange(slots, dtype=jnp.int32) < pair_count[0]
    user_counts = histogram(jnp.where(keep, pair_user, -1), users)
    item_counts = histogram(jnp.where(rows >= 0, cols, -1), items)
    keep_half, give_half = grams(flag, user_counts, item_counts, user_table, item_table)
    mine = keep_half + swap(give_half)
    mine = chip_scatter(mine.reshape(64, 72, NB))
    packed = chip_gather(mine).reshape(36 * NB, NB)

    spot = jnp.where(rows >= 0, rows, users)
    ct = cross(flag, spot, cols, item_table, (user_table,), (1,), 0)
    ct = cross(flag, spot, cols, item_table, (left, right), (1, 1), 1, ct)
    half, give = cross(flag, spot, cols, item_table, (far_a, far_b), (2,), 3, ct, halves=True)
    half = half + swap(give)
    ct = chip_scatter(half.reshape(64, 8, width))

    mine = chol(packed, 1.0 / total)
    other = swap(mine)
    r_user, left = thin(flag, ct, mine, other, 0, float(total) ** -0.5)
    left = lax.all_to_all(left, CORE_FIRST, 0, 0, tiled=True).reshape(width, NB)
    r_item, whitened = thin(flag, left, mine, other, 1)
    return (r_user, r_item, whitened)


def solution(mesh):
    fine = Mesh(mesh.devices.reshape(4, 4, 2, 4), ALL)
    placed = (P(ALL, None), P("x", None), P(ALL), P(ALL), P(ALL), P(ALL))

    return jax.shard_map(
        body,
        mesh=fine,
        in_specs=placed,
        out_specs=(P(), P(), P(ALL, None)),
        check_vma=False,
    )
```
